512 devices in a mesh: dp: 8 (over x, core), seq: 64 (over z, y).
Axes of the slice: x: 4, y: 8, z: 8, core: 2. Of those that a mesh axis runs over, the one named last changes fastest.
Arguments:
- queries: bfloat16 [8, 8192, 2048], P('dp', 'seq'), may hold values from -6 to 6
- keys: bfloat16 [8, 8192, 2048], P('dp', 'seq'), may hold values from -0.75 to 0.75
- values: bfloat16 [8, 8192, 2048], P('dp', 'seq'), may hold values from -6 to 6
- log_decay: float32 [8, 32, 8192], P('dp', None, 'seq'), may hold values from -0.7 to 0
- gain: float32 [2048], replicated, may hold values from 0.25 to 1.75
- d_out: bfloat16 [8, 8192, 2048], P('dp', 'seq'), may hold values from -12 to 12
Outputs:
- d_queries: bfloat16 [8, 8192, 2048], P('dp', 'seq')
- d_keys: bfloat16 [8, 8192, 2048], P('dp', 'seq')
- d_values: bfloat16 [8, 8192, 2048], P('dp', 'seq')
- d_log_decay: float32 [8, 32, 8192], P('dp', None, 'seq')
- d_gain: float32 [2048], replicated
The draws below stay inside these ranges and needn't reach their ends.
All inputs are finite; a program needn't handle non-finite values.
Results may differ from the reference program's by a relative error of at most 0.001.
Values sent between devices are 32-bit elements; how exact they have to be, the bound alone decides.
No kernel may reach another device: no remote copies, remote signals or barrier semaphores. Data moves between devices by JAX's collectives and lax.ppermute only.
A program may use at most 192 MiB of HBM per device.

```python
import math
import jax
import jax.numpy as jnp
from jax import lax

ATTENTION_HEADS = 32
HEAD = 64
TOK_DEV = 128
SEQUENCE_LENGTH = 8192
BATCH_SEQUENCES = 8
N_SEQ = 64


def draw_log_decay(key, part):
    random_key_variety, random_key_gradual, random_key_quick, random_key_coarse, random_key_location, random_key_spike = jax.random.split(key, 6)
    kind = jax.random.randint(random_key_variety, (1, ATTENTION_HEADS, 1), 0, 2) > 0
    slow = jnp.exp(jax.random.uniform(random_key_gradual, (1, ATTENTION_HEADS, 1), jnp.float32, math.log(0.05), math.log(0.3))) / SEQUENCE_LENGTH
    fast = jnp.exp(jax.random.uniform(random_key_quick, (1, ATTENTION_HEADS, 1), jnp.float32, math.log(0.02), math.log(0.033)))
    decay_speed = jnp.where(kind, slow, fast)
    coarse_values = jnp.exp(jax.random.uniform(random_key_coarse, (BATCH_SEQUENCES, ATTENTION_HEADS, SEQUENCE_LENGTH), jnp.float32, math.log(0.5), math.log(2.0)))
    places = jax.random.randint(random_key_location, (BATCH_SEQUENCES, ATTENTION_HEADS, 2), 0, SEQUENCE_LENGTH)
    spots = jnp.arange(SEQUENCE_LENGTH)[None, None, :, None] == places[:, :, None, :]
    hit_positions = jnp.any(spots, axis=3)
    sudden_spike = jnp.log(jax.random.uniform(random_key_spike, (BATCH_SEQUENCES, ATTENTION_HEADS, SEQUENCE_LENGTH), jnp.float32, 0.5, 0.8))
    return jnp.where(hit_positions, sudden_spike, -decay_speed * coarse_values).astype(jnp.float32)


def draw_d_out(key, part):
    key_base = jax.random.fold_in(key, 0)
    ramp = 1.0 + 2.0 * jnp.arange(SEQUENCE_LENGTH, dtype=jnp.float32)[None, :, None] / SEQUENCE_LENGTH
    base = jax.random.normal(key_base, (BATCH_SEQUENCES, SEQUENCE_LENGTH, ATTENTION_HEADS * HEAD), jnp.float32)
    return (jnp.clip(base, -4.0, 4.0) * ramp).astype(jnp.bfloat16)


def block_scale(stream_key, shape, cuts, low, largest):
    def one(dim, blocks):
        steps = jax.random.uniform(jax.random.fold_in(jax.random.fold_in(stream_key, 6), dim), (blocks,), jnp.float32, low / len(cuts), largest / len(cuts))
        return jnp.repeat(jnp.exp(steps), shape[dim] // blocks).reshape((-1,) + (1,) * (len(shape) - dim - 1))

    level = one(*cuts[0])
    for cut in cuts[1:]:
        level = level * one(*cut)
    return level


def scatter_about(key, extent, scale, reach, pieces=(), kind=jnp.bfloat16):
    result = jax.random.normal(key, extent, jnp.float32) * scale
    if len(pieces) > 0:
        result = block_scale(key, extent, pieces, -0.22, 0.18) * result
    return jnp.clip(result, min=-reach, max=reach).astype(kind)


def setup_inputs(seed: int = 0) -> dict:
    arg_keys = jax.random.split(jax.random.key(seed), 7)
    return {
        "queries": scatter_about(arg_keys[0], (BATCH_SEQUENCES, SEQUENCE_LENGTH, ATTENTION_HEADS * HEAD), 1.0, 6.0, ((0, 8), (1, 64))),
        "keys": scatter_about(arg_keys[1], (BATCH_SEQUENCES, SEQUENCE_LENGTH, ATTENTION_HEADS * HEAD), HEAD ** -0.5, 0.75, ((0, 8), (1, 64))),
        "values": scatter_about(arg_keys[2], (BATCH_SEQUENCES, SEQUENCE_LENGTH, ATTENTION_HEADS * HEAD), 1.0, 6.0, ((0, 8), (1, 64))),
        "log_decay": draw_log_decay(jax.random.fold_in(arg_keys[6], 71), 0),
        "gain": jnp.clip(1.0 + 0.15 * jax.random.normal(arg_keys[4], (ATTENTION_HEADS * HEAD,), jnp.float32), 0.25, 1.75),
        "d_out": draw_d_out(jax.random.fold_in(arg_keys[6], 71), 0),
    }


HIGH = lax.Precision.HIGHEST
EPSILON = 1e-06

def decay_table(log_block):
    cumulative = jnp.cumsum(log_block, axis=1)
    spread = cumulative[:, :, None] - cumulative[:, None, :]
    length = log_block.shape[1]
    lower = jnp.arange(length)[:, None] >= jnp.arange(length)[None, :]
    table = jnp.where(lower[None], jnp.exp(jnp.minimum(spread, 0.0)), 0.0)
    return (cumulative, table)

def block_out(query, keys, values, log_block, start_state):
    cumulative, table = decay_table(log_block)
    scores = jnp.einsum('htd,hsd->hts', query, keys, precision=HIGH) * table
    inside = jnp.einsum('hts,hse->hte', scores, values, precision=HIGH)
    carried = jnp.einsum('htd,hde->hte', query, start_state, precision=HIGH)
    return inside + jnp.exp(cumulative)[:, :, None] * carried

def block_end(keys, values, log_block, start_state):
    cumulative = jnp.cumsum(log_block, axis=1)
    total = cumulative[:, -1]
    weighted = keys * jnp.exp(total[:, None] - cumulative)[:, :, None]
    fresh = jnp.einsum('hsd,hse->hde', weighted, values, precision=HIGH)
    return jnp.exp(total)[:, None, None] * start_state + fresh

def normalize(attended, gain):
    heads, length, width = attended.shape
    flat = jnp.transpose(attended, (1, 0, 2)).reshape(length, heads * width)
    scale = jnp.sqrt(lax.optimization_barrier(jnp.mean(flat * flat, axis=1, keepdims=True)) + EPSILON)
    return flat / scale * gain

def forward(query, keys, values, log_decay, gain):

    def advance(state, item):
        query_block, key_block, value_block, log_block = item
        attended = block_out(query_block, key_block, value_block, log_block, state)
        return (block_end(key_block, value_block, log_block, state), normalize(attended, gain))
    start = jnp.zeros((ATTENTION_HEADS, HEAD, HEAD), jnp.float32)
    _, normed = lax.scan(advance, start, (query, keys, values, log_decay))
    return normed

def to_heads(array):
    shaped = array.astype(jnp.float32).reshape(N_SEQ, TOK_DEV, ATTENTION_HEADS, HEAD)
    return jnp.transpose(shaped, (0, 2, 1, 3))

def from_heads(array):
    return jnp.transpose(array, (0, 2, 1, 3)).reshape(N_SEQ * TOK_DEV, ATTENTION_HEADS * HEAD).astype(jnp.bfloat16)

def reference(queries, keys, values, log_decay, gain, d_out):

    def one_sequence(item):
        query, key_seq, value_seq, log_seq, cotangent = item
        log_blocks = jnp.transpose(log_seq.reshape(ATTENTION_HEADS, N_SEQ, TOK_DEV), (1, 0, 2))
        _, pull = jax.vjp(forward, to_heads(query), to_heads(key_seq), to_heads(value_seq), log_blocks, gain)
        grads = pull(cotangent.astype(jnp.float32).reshape(N_SEQ, TOK_DEV, ATTENTION_HEADS * HEAD))
        d_log = jnp.transpose(grads[3], (1, 0, 2)).reshape(ATTENTION_HEADS, N_SEQ * TOK_DEV)
        return (from_heads(grads[0]), from_heads(grads[1]), from_heads(grads[2]), d_log, grads[4])
    d_queries, d_keys, d_values, d_log_decay, gains = lax.map(one_sequence, (queries, keys, values, log_decay, d_out))
    return (d_queries, d_keys, d_values, d_log_decay, lax.optimization_barrier(jnp.sum(gains, axis=0)))
```

```python
import jax
import jax.numpy as jnp
from jax import lax
from jax.experimental import pallas as pl
from jax.experimental.pallas import tpu as pltpu
from jax.sharding import PartitionSpec as P

HIGH = lax.Precision.HIGHEST
EPSILON = 1e-06
F32 = jnp.float32
BF16 = jnp.bfloat16
LANES = 128
NN = (((1,), (0,)), ((), ()))
NT = (((1,), (1,)), ((), ()))
TN = (((0,), (0,)), ((), ()))


def mm(a, b, dims=NN):
    return lax.dot_general(a, b, dims, preferred_element_type=F32)


def exact(a, b, dims=NN):
    return lax.dot_general(a, b, dims, precision=HIGH, preferred_element_type=F32)


def iota(shape, axis):
    return lax.broadcasted_iota(jnp.int32, shape, axis)


def halves(x):
    hi = x.astype(BF16)
    return hi, (x - hi.astype(F32)).astype(BF16)


def thirds(x):
    hi = x.astype(BF16)
    rest = x - hi.astype(F32)
    mid = rest.astype(BF16)
    return hi, mid, (rest - mid.astype(F32)).astype(BF16)


def expand(x, width, store):
    heads = x.shape[1]
    parts = thirds(x)
    for start in range(0, heads * width, 256):
        pick = (iota((heads, 256), 0) == (iota((heads, 256), 1) + start) // width).astype(F32).astype(BF16)
        store(start, sum(mm(part, pick) for part in parts))


def side(width):
    lane = iota((1, width), 1) & (LANES - 1)
    first = jnp.where(lane < LANES // 2, 1.0, 0.0).astype(F32)
    return first.astype(BF16), (1.0 - first).astype(BF16)


def stacked(x, m0, m1):
    return jnp.concatenate([x * m0, x * m1], axis=0)


def compact(full):
    lane = iota((LANES // 2, LANES), 1)
    return jnp.where(lane < LANES // 2, full[: LANES // 2], full[LANES // 2 :])


def sums(log, length):
    row, col = iota((length, length), 0), iota((length, length), 1)
    cumulative_t = exact((col <= row).astype(F32), log, NT)
    return cumulative_t, cumulative_t[length - 1 : length]


def fresh_kernel(k_ref, v_ref, log_ref, out_ref, weight):
    length, features = k_ref.shape
    pairs = features // LANES
    cumulative_t, total = sums(log_ref[...], length)

    def store(start, value):
        weight[:, start : start + 256] = value

    expand(
        jnp.concatenate(
            [jnp.exp(total - cumulative_t), jnp.broadcast_to(jnp.exp(total), (8, total.shape[1]))], 0
        ),
        64,
        store,
    )
    for p in range(pairs):
        lanes = slice(p * LANES, (p + 1) * LANES)
        k_t = k_ref[:, lanes].T
        hi, lo = halves(weight[:length, lanes] * v_ref[:, lanes].astype(F32))
        state = compact(mm(jnp.concatenate([k_t, k_t], 1), jnp.concatenate([hi, lo], 0)))
        decay = weight[length : length + 1, lanes]
        for i in range(4):
            j = 17 * (4 * p + i)
            out_ref[j : j + 16] = state[16 * i : 16 * i + 16]
            out_ref[j + 16 : j + 17] = decay


def scan_kernel(in_ref, out_ref, decay_ref):
    count = decay_ref.shape[0]
    state = jnp.zeros((16, LANES), F32)
    for m in range(count):
        out_ref[16 * m : 16 * m + 16] = state
        decay = in_ref[17 * m + 16 : 17 * m + 17]
        decay_ref[m : m + 1] = decay
        state = decay * state + in_ref[17 * m : 17 * m + 16]


def gain_kernel(in_ref, out_ref):
    count = in_ref.shape[0] // 17
    total = in_ref[16:17]
    for m in range(1, count):
        total = total + in_ref[17 * m + 16 : 17 * m + 17]
    out_ref[...] = jnp.broadcast_to(total[None], out_ref.shape)


def back_kernel(in_ref, decay_ref, gain_ref, out_ref):
    count = decay_ref.shape[0]
    gain = gain_ref[0, 0:1]
    for i in range(1, gain_ref.shape[0]):
        gain = gain + gain_ref[i, 0:1]
    state = jnp.zeros((16, LANES), F32)
    for m in range(count - 1, -1, -1):
        out_ref[17 * m : 17 * m + 16] = state
        out_ref[17 * m + 16 : 17 * m + 17] = gain
        state = decay_ref[m : m + 1] * state + in_ref[17 * m : 17 * m + 16]


def main_kernel(
    q_ref, k_ref, v_ref, g_ref, log_ref, gain_ref, state_ref,
    dq_ref, out_ref, dk_ref, dv_ref, z_ref,
    cum, cum_wide, grow, table, att, inner, gains,
):
    length, features = q_ref.shape
    heads = log_ref.shape[0]
    pairs = features // LANES
    log = log_ref[...]
    row, col = iota((length, length), 0), iota((length, length), 1)
    cum[...] = exact(log, (row <= col).astype(F32))
    cumulative_t, _ = sums(log, length)

    def store_wide(start, value):
        cum_wide[:, start : start + 256] = value

    def store_grow(start, value):
        grow[:, start : start + 256] = value

    expand(cumulative_t, LANES, store_wide)
    expand(jnp.exp(cumulative_t), 64, store_grow)
    m0, m1 = side(LANES)
    lower = row >= col
    upper = row <= col

    def block_diagonal(p):
        hi, lo = halves(state_ref[pl.ds(pl.multiple_of(p * 64, 64), 64), :])
        return stacked(hi, m0, m1), stacked(lo, m0, m1)

    def pair(p):
        return pl.ds(pl.multiple_of(p * LANES, LANES), LANES)

    def attend(p, carry):
        square, dot = carry
        lanes = pair(p)
        q, k, v = q_ref[:, lanes], k_ref[:, lanes], v_ref[:, lanes]
        score = mm(q, stacked(k, m0, m1), NT)
        decays = []
        for a in range(2):
            wide = cum_wide[:, pl.ds(pl.multiple_of((2 * p + a) * LANES, LANES), LANES)]
            spread = jnp.minimum(wide - cum[pl.ds(2 * p + a, 1), :], 0.0)
            decays.append(jnp.where(lower, jnp.exp(spread), 0.0))
        decay = jnp.concatenate(decays, 1)
        table[pl.ds(pl.multiple_of(p * LANES, LANES), LANES), :] = decay
        hi, lo = halves(score * decay)
        both = stacked(v, m0, m1)
        inside = mm(hi, both) + mm(lo, both)
        state_hi, state_lo = block_diagonal(p)
        carried = mm(jnp.concatenate([q, q], 1), jnp.concatenate([state_hi, state_lo], 0))
        attended = inside + grow[:, lanes] * carried
        att[:, lanes] = attended
        weighted = gain_ref[:, lanes] * g_ref[:, lanes].astype(F32)
        return square + attended * attended, dot + attended * weighted

    zero = jnp.zeros((length, LANES), F32)
    square, dot = lax.fori_loop(0, pairs, attend, (zero, zero))
    scale = jnp.sqrt(jnp.sum(square, 1, keepdims=True) / features + EPSILON)
    inverse = 1.0 / scale
    slope = jnp.sum(dot, 1, keepdims=True) * (inverse * inverse * inverse) / features
    z_ref[...] = jnp.zeros_like(z_ref)

    def pull(p, carry):
        lanes = pair(p)
        q, k, v = q_ref[:, lanes], k_ref[:, lanes], v_ref[:, lanes]
        attended = att[:, lanes]
        g = g_ref[:, lanes].astype(F32) * inverse
        gains[pl.ds(p, 1), :] = jnp.sum(g * attended, 0, keepdims=True)
        x = gain_ref[:, lanes] * g - attended * slope
        x_hi, x_lo = halves(x)
        y_hi, y_lo = halves(grow[:, lanes] * x)
        k2, q2, v2 = stacked(k, m0, m1), stacked(q, m0, m1), stacked(v, m0, m1)
        x2_hi, x2_lo = stacked(x_hi, m0, m1), stacked(x_lo, m0, m1)
        d_weight = mm(jnp.concatenate([x_hi, x_lo], 1), jnp.concatenate([v2, v2], 1), NT)
        hi, lo = halves(d_weight * table[pl.ds(pl.multiple_of(p * LANES, LANES), LANES), :])
        state_hi, state_lo = block_diagonal(p)
        dq = mm(hi, k2) + mm(lo, k2) + mm(y_hi, state_lo, NT)
        dq = dq + mm(jnp.concatenate([y_hi, y_lo], 1), jnp.concatenate([state_hi, state_hi], 1), NT)
        dq_ref[:, lanes] = dq.astype(BF16)
        decays = []
        for a in range(2):
            wide = cum_wide[:, pl.ds(pl.multiple_of((2 * p + a) * LANES, LANES), LANES)]
            spread = jnp.minimum(cum[pl.ds(2 * p + a, 1), :] - wide, 0.0)
            decays.append(jnp.where(upper, jnp.exp(spread), 0.0))
        decay = jnp.concatenate(decays, 1)
        hi, lo = halves(mm(k, q2, NT) * decay)
        dv_ref[:, lanes] = mm(hi, x2_hi) + mm(lo, x2_hi) + mm(hi, x2_lo)
        d_weight = mm(jnp.concatenate([v, v], 1), jnp.concatenate([x2_hi, x2_lo], 1), NT)
        hi, lo = halves(d_weight * decay)
        dk = mm(hi, q2) + mm(lo, q2)
        dk_ref[:, lanes] = dk
        q_t = q.T
        full = mm(jnp.concatenate([q_t, q_t], 1), jnp.concatenate([y_hi, y_lo], 0))
        inner[pl.ds(pl.multiple_of(p * 64, 64), 64), :] = compact(full)
        hi, lo = halves(q.astype(F32) * dq - k.astype(F32) * dk)
        z_ref[...] += mm(picker(heads, p), jnp.concatenate([hi, lo], 1), NT)
        return carry

    lax.fori_loop(0, pairs, pull, 0)
    for j in range(4 * pairs):
        out_ref[17 * j : 17 * j + 16] = inner[16 * j : 16 * j + 16]
        out_ref[17 * j + 16 : 17 * j + 17] = gains[j // 4 : j // 4 + 1]


def picker(heads, p):
    lane = iota((heads, 2 * LANES), 1) & (LANES - 1)
    head = 2 * p + lane // 64
    return (iota((heads, 2 * LANES), 0) == head).astype(F32).astype(BF16)


def last_kernel(
    k_ref, v_ref, log_ref, state_ref, dk_in, dv_in, z_ref, in_ref,
    dk_ref, dv_ref, log_out, gain_out,
    weight, inner, kept,
):
    length, features = k_ref.shape
    heads = log_ref.shape[0]
    pairs = features // LANES
    log = log_ref[...]
    cumulative_t, total = sums(log, length)

    def store(start, value):
        weight[:, start : start + 256] = value

    expand(jnp.exp(total - cumulative_t), 64, store)
    for j in range(4 * pairs):
        inner[16 * j : 16 * j + 16] = in_ref[17 * j : 17 * j + 16]
    for p in range(pairs):
        gain_out[p : p + 1] = in_ref[17 * 4 * p + 16 : 17 * 4 * p + 17]
    m0, m1 = side(LANES)
    lane = iota((1, LANES), 1)

    def finish(p, u):
        lanes = pl.ds(pl.multiple_of(p * LANES, LANES), LANES)
        rows = pl.ds(pl.multiple_of(p * 64, 64), 64)
        k, v = k_ref[:, lanes], v_ref[:, lanes]
        grad = inner[rows, :]
        hi, lo = halves(grad)
        hi, lo = stacked(hi, m0, m1), stacked(lo, m0, m1)
        w = weight[:, lanes]
        dk = w * mm(jnp.concatenate([v, v], 1), jnp.concatenate([hi, lo], 1), NT)
        dv = w * mm(jnp.concatenate([k, k], 1), jnp.concatenate([hi, lo], 0))
        dk_ref[:, lanes] = (dk_in[:, lanes] + dk).astype(BF16)
        dv_ref[:, lanes] = (dv_in[:, lanes] + dv).astype(BF16)
        part = jnp.sum(grad * state_ref[rows, :], 0, keepdims=True)
        kept[pl.ds(2 * p, 1), :] = jnp.where(lane < 64, part, 0.0)
        kept[pl.ds(2 * p + 1, 1), :] = jnp.where(lane < 64, 0.0, part)
        hi, lo = halves(k.astype(F32) * dk)
        return u + mm(picker(heads, p), jnp.concatenate([hi, lo], 1), NT)

    u = lax.fori_loop(0, pairs, finish, jnp.zeros((heads, length), F32))
    row, col = iota((length, length), 0), iota((length, length), 1)
    whole = jnp.exp(jnp.sum(log, 1, keepdims=True)) * jnp.sum(kept[...], 1, keepdims=True)
    log_out[...] = (
        exact(z_ref[...], (row >= col).astype(F32)) + exact(u, (row < col).astype(F32)) + whole
    )


def call(kernel, outs, scratch, flops, *args):
    vmem = pl.BlockSpec(memory_space=pltpu.VMEM)
    outs = [jax.ShapeDtypeStruct(shape, dtype) for shape, dtype in outs]
    size = sum(a.size * a.dtype.itemsize for a in [*args, *outs])
    return pl.pallas_call(
        kernel,
        out_shape=outs,
        in_specs=[vmem] * len(args),
        out_specs=[vmem] * len(outs),
        scratch_shapes=[pltpu.VMEM(shape, dtype) for shape, dtype in scratch],
        cost_estimate=pl.CostEstimate(flops=flops, bytes_accessed=size, transcendentals=0),
        compiler_params=pltpu.CompilerParams(vmem_limit_bytes=48 << 20),
    )(*args)


def exchange(array, axis):
    count = lax.axis_size(axis)
    rows, lanes = array.shape
    pieces = array.reshape(count, 1, rows // count * lanes)
    return lax.all_to_all(pieces, axis, 0, 0, tiled=True).reshape(rows, lanes)


def shards(queries, keys, values, log_decay, gain, d_out):
    length, features = queries.shape[1:]
    heads = log_decay.shape[1]
    pairs = features // LANES
    count = lax.axis_size("seq")
    assert features == 32 * count and features == 64 * heads and length == LANES
    q, k, v, g, log = queries[0], keys[0], values[0], d_out[0], log_decay[0]
    wide = (length, features)
    sent = (17 * count, LANES)
    states = (16 * count, LANES)

    (fresh,) = call(fresh_kernel, [(sent, F32)], [((length + 8, features), F32)], 1 << 27, k, v, log)
    begun, decays = call(
        scan_kernel, [(states, F32), ((count, LANES), F32)], [], 1 << 20, exchange(fresh, "seq")
    )
    start = exchange(begun, "seq")
    d_queries, incoming, dk, dv, z = call(
        main_kernel,
        [(wide, BF16), (sent, F32), (wide, F32), (wide, F32), ((heads, length), F32)],
        [
            ((heads, length), F32),
            ((length, heads * LANES), F32),
            (wide, F32),
            ((features, 2 * LANES), F32),
            (wide, F32),
            (states, F32),
            ((pairs, LANES), F32),
        ],
        1 << 30,
        q, k, v, g, log, gain[None], start,
    )
    arrived = exchange(incoming, "seq")
    groups = lax.axis_size("dp")
    (partial,) = call(gain_kernel, [((groups, 8, LANES), F32)], [], 1 << 10, arrived)
    partial = lax.all_to_all(partial, "dp", 0, 0, tiled=True)
    (ended,) = call(back_kernel, [(sent, F32)], [], 1 << 20, arrived, decays, partial)
    d_keys, d_values, d_log, d_gain = call(
        last_kernel,
        [(wide, BF16), (wide, BF16), ((heads, length), F32), ((pairs, LANES), F32)],
        [(wide, F32), (states, F32), ((heads, LANES), F32)],
        1 << 28,
        k, v, log, start, dk, dv, z, exchange(ended, "seq"),
    )
    return d_queries[None], d_keys[None], d_values[None], d_log[None], d_gain.reshape(features)


def solution(mesh):
    tokens, decays = P("dp", "seq", None), P("dp", None, "seq")
    return jax.shard_map(
        shards,
        mesh=mesh,
        in_specs=(tokens, tokens, tokens, decays, P(), tokens),
        out_specs=(tokens, tokens, tokens, decays, P()),
        check_vma=False,
    )
```

```python
import math

import jax
import jax.numpy as jnp
from jax import lax
from jax.experimental import pallas as pl
from jax.experimental.pallas import tpu as pltpu
from jax.sharding import PartitionSpec as P

HIGH = lax.Precision.HIGHEST
EPSILON = 1e-06
F32 = jnp.float32
BF16 = jnp.bfloat16
LANES = 128
NN = (((1,), (0,)), ((), ()))
NT = (((1,), (1,)), ((), ()))
TN = (((0,), (0,)), ((), ()))


def mm(a, b, dims=NN):
    return lax.dot_general(a, b, dims, preferred_element_type=F32)


def exact(a, b, dims=NN):
    return lax.dot_general(a, b, dims, precision=HIGH, preferred_element_type=F32)


def iota(shape, axis):
    return lax.broadcasted_iota(jnp.int32, shape, axis)


def halves(x):
    hi = x.astype(BF16)
    return hi, (x - hi.astype(F32)).astype(BF16)


def thirds(x):
    hi = x.astype(BF16)
    rest = x - hi.astype(F32)
    mid = rest.astype(BF16)
    return hi, mid, (rest - mid.astype(F32)).astype(BF16)


def expand(x, width, store):
    heads = x.shape[1]
    parts = thirds(x)
    for start in range(0, heads * width, 256):
        pick = (iota((heads, 256), 0) == (iota((heads, 256), 1) + start) // width).astype(F32).astype(BF16)
        store(start, sum(mm(part, pick) for part in parts))


def side(width):
    lane = iota((1, width), 1) & (LANES - 1)
    first = jnp.where(lane < LANES // 2, 1.0, 0.0).astype(F32)
    return first.astype(BF16), (1.0 - first).astype(BF16)


def stacked(x, m0, m1):
    return jnp.concatenate([x * m0, x * m1], axis=0)


def compact(full):
    lane = iota((LANES // 2, LANES), 1)
    return jnp.where(lane < LANES // 2, full[: LANES // 2], full[LANES // 2 :])


def sums(log, length):
    row, col = iota((length, length), 0), iota((length, length), 1)
    cumulative_t = exact((col <= row).astype(F32), log, NT)
    return cumulative_t, cumulative_t[length - 1 : length]


def pair(p):
    return slice(p * LANES, (p + 1) * LANES)


def block_diagonal(state, m0, m1):
    hi, lo = halves(state)
    return stacked(hi, m0, m1), stacked(lo, m0, m1)


def decay_pair(wide_ref, cum_ref, p, keep, sign):
    parts = []
    for h in (2 * p, 2 * p + 1):
        spread = wide_ref[:, pair(h)] - cum_ref[h : h + 1, :]
        parts.append(jnp.where(keep, jnp.exp(jnp.minimum(sign * spread, 0.0)), 0.0))
    return jnp.concatenate(parts, 1)


def writer(ref):
    def store(start, value):
        ref[:, start : start + 256] = value

    return store


def send_state(out_ref, p, state, row):
    for i in range(4):
        j = 17 * (4 * p + i)
        out_ref[j : j + 16] = state[16 * i : 16 * i + 16]
        out_ref[j + 16 : j + 17] = row


def fresh_kernel(ready, emit, log_ref, k_ref, v_ref, out_ref, weight):
    length, features = k_ref.shape
    ready("log")
    cumulative_t, total = sums(log_ref[...], length)
    ends = jnp.broadcast_to(jnp.exp(total), (8, total.shape[1]))
    expand(jnp.concatenate([jnp.exp(total - cumulative_t), ends], 0), 64, writer(weight))
    for p in range(features // LANES):
        if p % 4 == 0:
            ready(p // 4)
        lanes = pair(p)
        k_t = k_ref[:, lanes].T
        hi, lo = halves(weight[:length, lanes] * v_ref[:, lanes].astype(F32))
        state = compact(mm(jnp.concatenate([k_t, k_t], 1), jnp.concatenate([hi, lo], 0)))
        send_state(out_ref, p, state, weight[length : length + 1, lanes])
        if p % 4 == 3:
            emit(p // 4)


def scan_kernel(in_ref, out_ref, decay_ref):
    count = decay_ref.shape[0]
    state = jnp.zeros((16, LANES), F32)
    for m in range(count):
        out_ref[16 * m : 16 * m + 16] = state
        decay = in_ref[17 * m + 16 : 17 * m + 17]
        decay_ref[m : m + 1] = decay
        state = decay * state + in_ref[17 * m : 17 * m + 16]


def back_kernel(in_ref, decay_ref, out_ref):
    count = decay_ref.shape[0]
    gain = in_ref[16:17]
    for m in range(1, count):
        gain = gain + in_ref[17 * m + 16 : 17 * m + 17]
    state = jnp.zeros((16, LANES), F32)
    for m in range(count - 1, -1, -1):
        out_ref[17 * m : 17 * m + 16] = state
        out_ref[17 * m + 16 : 17 * m + 17] = gain
        state = decay_ref[m : m + 1] * state + in_ref[17 * m : 17 * m + 16]


def gain_kernel(in_ref, out_ref, rows, sems):
    pairs = rows.shape[0]

    def copy(p):
        row = pl.ds(17 * 4 * p + 16, 1)
        return pltpu.make_async_copy(in_ref.at[row, :], rows.at[pl.ds(p, 1), :], sems.at[p])

    for p in range(pairs):
        copy(p).start()
    for p in range(pairs):
        copy(p).wait()
    out_ref[...] = jnp.broadcast_to(rows[...][None], out_ref.shape)


def gain_sum_kernel(in_ref, out_ref):
    total = in_ref[0]
    for d in range(1, in_ref.shape[0]):
        total = total + in_ref[d]
    out_ref[...] = total


def inside_kernel(
    ready, emit, log_ref, q_ref, k_ref, v_ref, cum_ref, wide_ref, grow_ref, weight_ref, inside_ref
):
    length, features = q_ref.shape
    ready("log")
    log = log_ref[...]
    row, col = iota((length, length), 0), iota((length, length), 1)
    cum_ref[...] = exact(log, (row <= col).astype(F32))
    cumulative_t, total = sums(log, length)
    expand(cumulative_t, LANES, writer(wide_ref))
    expand(jnp.exp(cumulative_t), 64, writer(grow_ref))
    expand(jnp.exp(total - cumulative_t), 64, writer(weight_ref))
    m0, m1 = side(LANES)
    for p in range(features // LANES):
        if p % 4 == 0:
            ready(p // 4)
        lanes = pair(p)
        score = mm(q_ref[:, lanes], stacked(k_ref[:, lanes], m0, m1), NT)
        hi, lo = halves(score * decay_pair(wide_ref, cum_ref, p, row >= col, 1.0))
        both = stacked(v_ref[:, lanes], m0, m1)
        inside_ref[:, lanes] = mm(hi, both) + mm(lo, both)
        if p % 4 == 3:
            emit(p // 4)


def middle_kernel(
    ready, emit, gain_ref, q_ref, g_ref, state_ref, grow_ref, inside_ref, out_ref, x_ref, att
):
    length, features = q_ref.shape
    pairs = features // LANES
    m0, m1 = side(LANES)
    square = dot = jnp.zeros((length, LANES), F32)
    ready("gain")
    for p in range(pairs):
        if p % 4 == 0:
            ready(p // 4)
        lanes = pair(p)
        q = q_ref[:, lanes]
        state_hi, state_lo = block_diagonal(state_ref[64 * p : 64 * p + 64], m0, m1)
        carried = mm(jnp.concatenate([q, q], 1), jnp.concatenate([state_hi, state_lo], 0))
        attended = inside_ref[:, lanes] + grow_ref[:, lanes] * carried
        att[:, lanes] = attended
        square = square + attended * attended
        dot = dot + attended * (gain_ref[:, lanes] * g_ref[:, lanes].astype(F32))
    scale = jnp.sqrt(jnp.sum(square, 1, keepdims=True) / features + EPSILON)
    inverse = 1.0 / scale
    slope = jnp.sum(dot, 1, keepdims=True) * (inverse * inverse * inverse) / features
    for p in range(pairs):
        lanes = pair(p)
        attended = att[:, lanes]
        g = g_ref[:, lanes].astype(F32) * inverse
        gain_row = jnp.sum(g * attended, 0, keepdims=True)
        x = gain_ref[:, lanes] * g - attended * slope
        x_ref[:, lanes] = x
        hi, lo = halves(grow_ref[:, lanes] * x)
        q_t = q_ref[:, lanes].T
        state = compact(mm(jnp.concatenate([q_t, q_t], 1), jnp.concatenate([hi, lo], 0)))
        send_state(out_ref, p, state, gain_row)
        if p % 4 == 3:
            emit(p // 4)


def local_kernel(
    ready, emit, cum_ref, q_ref, k_ref, v_ref, wide_ref, grow_ref, x_ref, state_ref,
    z_ref, dq_ref, dk_ref, dv_ref,
):
    length, features = q_ref.shape
    heads = cum_ref.shape[0]
    m0, m1 = side(LANES)
    row, col = iota((length, length), 0), iota((length, length), 1)
    z = jnp.zeros((heads, length), F32)
    ready("cum")
    for p in range(features // LANES):
        if p % 4 == 0:
            ready(p // 4)
        lanes = pair(p)
        q, k, v, x = q_ref[:, lanes], k_ref[:, lanes], v_ref[:, lanes], x_ref[:, lanes]
        x_hi, x_lo = halves(x)
        y_hi, y_lo = halves(grow_ref[:, lanes] * x)
        k2, q2, v2 = stacked(k, m0, m1), stacked(q, m0, m1), stacked(v, m0, m1)
        x2_hi, x2_lo = stacked(x_hi, m0, m1), stacked(x_lo, m0, m1)
        d_weight = mm(jnp.concatenate([x_hi, x_lo], 1), jnp.concatenate([v2, v2], 1), NT)
        hi, lo = halves(d_weight * decay_pair(wide_ref, cum_ref, p, row >= col, 1.0))
        state_hi, state_lo = block_diagonal(state_ref[64 * p : 64 * p + 64], m0, m1)
        dq = mm(hi, k2) + mm(lo, k2) + mm(y_hi, state_lo, NT)
        dq = dq + mm(jnp.concatenate([y_hi, y_lo], 1), jnp.concatenate([state_hi, state_hi], 1), NT)
        dq_ref[:, lanes] = dq.astype(BF16)
        decay = decay_pair(wide_ref, cum_ref, p, row <= col, -1.0)
        hi, lo = halves(mm(k, q2, NT) * decay)
        dv_ref[:, lanes] = mm(hi, x2_hi) + mm(lo, x2_hi) + mm(hi, x2_lo)
        d_weight = mm(jnp.concatenate([v, v], 1), jnp.concatenate([x2_hi, x2_lo], 1), NT)
        hi, lo = halves(d_weight * decay)
        dk = mm(hi, q2) + mm(lo, q2)
        dk_ref[:, lanes] = dk
        hi, lo = halves(q.astype(F32) * dq - k.astype(F32) * dk)
        z = z + mm(picker(heads, p), jnp.concatenate([hi, lo], 1), NT)
        if p % 4 == 3:
            emit(p // 4)
    z_ref[...] = z


def picker(heads, p):
    lane = iota((heads, 2 * LANES), 1) & (LANES - 1)
    head = 2 * p + lane // 64
    return (iota((heads, 2 * LANES), 0) == head).astype(F32).astype(BF16)


def last_kernel(
    ready, emit, log_ref, z_ref, in_ref, k_ref, v_ref, weight_ref, state_ref, dk_in, dv_in,
    log_out, dk_ref, dv_ref, kept,
):
    length, features = k_ref.shape
    heads = log_ref.shape[0]
    m0, m1 = side(LANES)
    lane = iota((1, LANES), 1)
    u = jnp.zeros((heads, length), F32)
    ready("log")
    ready("z")
    for p in range(features // LANES):
        if p % 4 == 0:
            ready(p // 4)
        lanes = pair(p)
        k, v, w = k_ref[:, lanes], v_ref[:, lanes], weight_ref[:, lanes]
        j = 17 * 4 * p
        grad = jnp.concatenate([in_ref[j + 17 * i : j + 17 * i + 16] for i in range(4)], 0)
        hi, lo = block_diagonal(grad, m0, m1)
        dk = w * mm(jnp.concatenate([v, v], 1), jnp.concatenate([hi, lo], 1), NT)
        dv = w * mm(jnp.concatenate([k, k], 1), jnp.concatenate([hi, lo], 0))
        dk_ref[:, lanes] = (dk_in[:, lanes] + dk).astype(BF16)
        dv_ref[:, lanes] = (dv_in[:, lanes] + dv).astype(BF16)
        part = jnp.sum(grad * state_ref[64 * p : 64 * p + 64], 0, keepdims=True)
        kept[2 * p : 2 * p + 1] = jnp.where(lane < 64, part, 0.0)
        kept[2 * p + 1 : 2 * p + 2] = jnp.where(lane < 64, 0.0, part)
        hi, lo = halves(k.astype(F32) * dk)
        u = u + mm(picker(heads, p), jnp.concatenate([hi, lo], 1), NT)
        if p % 4 == 3:
            emit(p // 4)
    row, col = iota((length, length), 0), iota((length, length), 1)
    whole = jnp.exp(jnp.sum(log_ref[...], 1, keepdims=True)) * jnp.sum(kept[...], 1, keepdims=True)
    log_out[...] = (
        exact(z_ref[...], (row >= col).astype(F32)) + exact(u, (row < col).astype(F32)) + whole
    )


def call(kernel, outs, flops, *args):
    vmem = pl.BlockSpec(memory_space=pltpu.VMEM)
    outs = [jax.ShapeDtypeStruct(shape, dtype) for shape, dtype in outs]
    size = sum(a.size * a.dtype.itemsize for a in [*args, *outs])
    return pl.pallas_call(
        kernel,
        out_shape=outs,
        in_specs=[vmem] * len(args),
        out_specs=[vmem] * len(outs),
        cost_estimate=pl.CostEstimate(flops=flops, bytes_accessed=size, transcendentals=0),
        compiler_params=pltpu.CompilerParams(vmem_limit_bytes=4 << 20),
    )(*args)


def staged(kernel, flops, limit, ins, outs, scratch=()):
    in_shapes = [(a.shape, a.dtype) for a in ins.values()]
    out_shapes = list(outs.values())
    names = [*ins, *outs]
    shapes = in_shapes + out_shapes
    small = [shape[0] <= 32 for shape, _ in shapes]
    count = len(shapes)

    def body(*refs):
        far, near = refs[:count], refs[count : 2 * count]
        sems, own = refs[2 * count], refs[2 * count + 1 :]

        def copy(i, c):
            rows, lanes = shapes[i][0]
            if small[i]:
                a, b = far[i], near[i]
            elif lanes == LANES:
                part = pl.ds(c * (rows // 4), rows // 4)
                a, b = far[i].at[part, :], near[i].at[part, :]
            else:
                part = pl.ds(c * (lanes // 4), lanes // 4)
                a, b = far[i].at[:, part], near[i].at[:, part]
            if i >= len(ins):
                a, b = b, a
            return pltpu.make_async_copy(a, b, sems.at[i, c])

        sent = range(len(ins), count)
        for i in range(len(ins)):
            if small[i]:
                copy(i, 0).start()
        for c in range(4):
            for i in range(len(ins)):
                if not small[i]:
                    copy(i, c).start()

        def ready(c):
            for i in range(len(ins)):
                if small[i] and names[i] == c:
                    copy(i, 0).wait()
                if not small[i] and c in range(4):
                    copy(i, c).wait()

        def emit(c):
            for i in sent:
                if not small[i]:
                    copy(i, c).start()

        kernel(ready, emit, *near, *own)
        for i in sent:
            if small[i]:
                copy(i, 0).start()
        for i in sent:
            for c in range(1 if small[i] else 4):
                copy(i, c).wait()

    hbm = pl.BlockSpec(memory_space=pltpu.HBM)
    results = [jax.ShapeDtypeStruct(shape, dtype) for shape, dtype in out_shapes]
    size = sum(math.prod(shape) * jnp.dtype(dtype).itemsize for shape, dtype in shapes)
    return pl.pallas_call(
        body,
        out_shape=results,
        in_specs=[hbm] * len(ins),
        out_specs=[hbm] * len(outs),
        scratch_shapes=[
            *(pltpu.VMEM(shape, dtype) for shape, dtype in shapes),
            pltpu.SemaphoreType.DMA((count, 4)),
            *(pltpu.VMEM(shape, dtype) for shape, dtype in scratch),
        ],
        cost_estimate=pl.CostEstimate(flops=flops, bytes_accessed=size, transcendentals=0),
        compiler_params=pltpu.CompilerParams(vmem_limit_bytes=limit << 20),
    )(*ins.values())


def exchange(array, axis):
    count = lax.axis_size(axis)
    rows, lanes = array.shape
    pieces = array.reshape(count, 1, rows // count * lanes)
    return lax.all_to_all(pieces, axis, 0, 0, tiled=True).reshape(rows, lanes)


def shards(queries, keys, values, log_decay, gain, d_out):
    length, features = queries.shape[1:]
    heads = log_decay.shape[1]
    pairs = features // LANES
    count = lax.axis_size("seq")
    assert features == 32 * count and features == 64 * heads and length == LANES
    q, k, v, g, log = queries[0], keys[0], values[0], d_out[0], log_decay[0]
    wide = ((length, features), F32)
    half = ((length, features), BF16)
    small = ((heads, length), F32)
    sent = ((17 * count, LANES), F32)

    (fresh,) = staged(
        fresh_kernel, 1 << 27, 60, dict(log=log, k=k, v=v), dict(out=sent),
        [((length + 8, features), F32)],
    )
    arrived = exchange(fresh, "seq")
    cum, spread, grow, weight, inside = staged(
        inside_kernel, 1 << 30, 60, dict(log=log, q=q, k=k, v=v),
        dict(cum=small, spread=((length, heads * LANES), F32), grow=wide, weight=wide, inside=wide),
    )
    arrived, inside = lax.optimization_barrier((arrived, inside))
    begun, decays = call(
        scan_kernel, [((16 * count, LANES), F32), ((count, LANES), F32)], 1 << 20, arrived
    )
    start = exchange(begun, "seq")
    incoming, x = staged(
        middle_kernel, 1 << 28, 60,
        dict(gain=gain[None], q=q, g=g, state=start, grow=grow, inside=inside),
        dict(out=sent, x=wide), [wide],
    )
    returned = exchange(incoming, "seq")
    z, d_queries, dk, dv = staged(
        local_kernel, 1 << 31, 60,
        dict(cum=cum, q=q, k=k, v=v, spread=spread, grow=grow, x=x, state=start),
        dict(z=small, dq=half, dk=wide, dv=wide),
    )
    returned, dk = lax.optimization_barrier((returned, dk))
    (ended,) = call(back_kernel, [sent], 1 << 20, returned, decays)
    ended = exchange(ended, "seq")
    shares = jax.ShapeDtypeStruct((lax.axis_size("dp"), pairs, LANES), F32)
    share = pl.pallas_call(
        gain_kernel,
        out_shape=shares,
        in_specs=[pl.BlockSpec(memory_space=pltpu.HBM)],
        out_specs=pl.BlockSpec(memory_space=pltpu.VMEM),
        scratch_shapes=[pltpu.VMEM((pairs, LANES), F32), pltpu.SemaphoreType.DMA((pairs,))],
        compiler_params=pltpu.CompilerParams(vmem_limit_bytes=60 << 20),
    )(ended)
    share = lax.all_to_all(share, "dp", 0, 0, tiled=True)
    (d_gain,) = call(gain_sum_kernel, [((pairs, LANES), F32)], 1 << 10, share)
    d_log, d_keys, d_values = staged(
        last_kernel, 1 << 28, 60,
        {"log": log, "z": z, "in": ended, "k": k, "v": v, "w": weight, "s": start, "dk": dk, "dv": dv},
        dict(log=small, dk=half, dv=half), [((heads, LANES), F32)],
    )
    return d_queries[None], d_keys[None], d_values[None], d_log[None], d_gain.reshape(features)


def solution(mesh):
    tokens, decays = P("dp", "seq", None), P("dp", None, "seq")
    return jax.shard_map(
        shards,
        mesh=mesh,
        in_specs=(tokens, tokens, tokens, decays, P(), tokens),
        out_specs=(tokens, tokens, tokens, decays, P()),
        check_vma=False,
    )
```

```python
import math

import jax
import jax.numpy as jnp
from jax import lax
from jax.experimental import pallas as pl
from jax.experimental.pallas import tpu as pltpu
from jax.sharding import PartitionSpec as P

HIGH = lax.Precision.HIGHEST
EPSILON = 1e-06
F32 = jnp.float32
BF16 = jnp.bfloat16
LANES = 128
PAIRS = 16
NN = (((1,), (0,)), ((), ()))
NT = (((1,), (1,)), ((), ()))
TN = (((0,), (0,)), ((), ()))


def mm(a, b, dims=NN):
    return lax.dot_general(a, b, dims, preferred_element_type=F32)


def exact(a, b, dims=NN):
    return lax.dot_general(a, b, dims, precision=HIGH, preferred_element_type=F32)


def iota(shape, axis):
    return lax.broadcasted_iota(jnp.int32, shape, axis)


def halves(x):
    hi = x.astype(BF16)
    return hi, (x - hi.astype(F32)).astype(BF16)


def columns(x, p):
    lane = iota((1, LANES), 1)
    return jnp.where(lane < LANES // 2, x[:, 2 * p : 2 * p + 1], x[:, 2 * p + 1 : 2 * p + 2])


def side(width):
    lane = iota((1, width), 1) & (LANES - 1)
    first = jnp.where(lane < LANES // 2, 1.0, 0.0).astype(F32)
    return first.astype(BF16), (1.0 - first).astype(BF16)


def stacked(x, m0, m1):
    return jnp.concatenate([x * m0, x * m1], axis=0)


def compact(full):
    lane = iota((LANES // 2, LANES), 1)
    return jnp.where(lane < LANES // 2, full[: LANES // 2], full[LANES // 2 :])


def sums(log, length):
    row, col = iota((length, length), 0), iota((length, length), 1)
    cumulative_t = exact((col <= row).astype(F32), log, NT)
    return cumulative_t, cumulative_t[length - 1 : length]


def pair(p):
    return slice(p * LANES, (p + 1) * LANES)


def block_diagonal(state, m0, m1):
    hi, lo = halves(state)
    return stacked(hi, m0, m1), stacked(lo, m0, m1)


def carry(q, state_hi, state_lo):
    return mm(jnp.concatenate([q, q], 1), jnp.concatenate([state_hi, state_lo], 0))


def decay_pair(cum_t, cum_ref, p, keep, sign):
    parts = []
    for h in (2 * p, 2 * p + 1):
        spread = cum_t[:, h : h + 1] - cum_ref[h : h + 1, :]
        parts.append(jnp.where(keep, jnp.exp(jnp.minimum(sign * spread, 0.0)), 0.0))
    return jnp.concatenate(parts, 1)


def send_state(out_ref, p, state, row):
    for i in range(4):
        j = 17 * (4 * p + i)
        out_ref[j : j + 16] = state[16 * i : 16 * i + 16]
        out_ref[j + 16 : j + 17] = row


def fresh_kernel(ready, emit, log_ref, k_ref, v_ref, out_ref):
    length, features = k_ref.shape
    ready("log")
    cumulative_t, total = sums(log_ref[...], length)
    weight, ends = jnp.exp(total - cumulative_t), jnp.exp(total)
    for p in range(features // LANES):
        ready(p)
        lanes = pair(p)
        k_t = k_ref[:, lanes].T
        hi, lo = halves(columns(weight, p) * v_ref[:, lanes].astype(F32))
        state = compact(mm(jnp.concatenate([k_t, k_t], 1), jnp.concatenate([hi, lo], 0)))
        send_state(out_ref, p, state, columns(ends, p))
        emit(p)


def scan_kernel(in_ref, out_ref, decay_ref):
    count = decay_ref.shape[0]
    state = jnp.zeros((16, LANES), F32)
    for m in range(count):
        out_ref[16 * m : 16 * m + 16] = state
        decay = in_ref[17 * m + 16 : 17 * m + 17]
        decay_ref[m : m + 1] = decay
        state = decay * state + in_ref[17 * m : 17 * m + 16]


def back_kernel(in_ref, decay_ref, out_ref):
    count = decay_ref.shape[0]
    gain = in_ref[16:17]
    for m in range(1, count):
        gain = gain + in_ref[17 * m + 16 : 17 * m + 17]
    state = jnp.zeros((16, LANES), F32)
    for m in range(count - 1, -1, -1):
        out_ref[17 * m : 17 * m + 16] = state
        out_ref[17 * m + 16 : 17 * m + 17] = gain
        state = decay_ref[m : m + 1] * state + in_ref[17 * m : 17 * m + 16]


def gain_kernel(in_ref, out_ref, rows, sems):
    pairs = rows.shape[0]

    def copy(p):
        row = pl.ds(17 * 4 * p + 16, 1)
        return pltpu.make_async_copy(in_ref.at[row, :], rows.at[pl.ds(p, 1), :], sems.at[p])

    for p in range(pairs):
        copy(p).start()
    for p in range(pairs):
        copy(p).wait()
    out_ref[...] = jnp.broadcast_to(rows[...][None], out_ref.shape)


def gain_sum_kernel(in_ref, out_ref):
    total = in_ref[0]
    for d in range(1, in_ref.shape[0]):
        total = total + in_ref[d]
    out_ref[...] = total


def inside_kernel(
    ready, emit, log_ref, q_ref, k_ref, v_ref, cum_ref, cum_t_ref, grow_ref, weight_ref, inside_ref
):
    length, features = q_ref.shape
    ready("log")
    log = log_ref[...]
    row, col = iota((length, length), 0), iota((length, length), 1)
    cum_ref[...] = exact(log, (row <= col).astype(F32))
    cumulative_t, total = sums(log, length)
    cum_t_ref[...] = cumulative_t
    grow_ref[...] = jnp.exp(cumulative_t)
    weight_ref[...] = jnp.exp(total - cumulative_t)
    m0, m1 = side(LANES)
    for p in range(features // LANES):
        ready(p)
        lanes = pair(p)
        score = mm(q_ref[:, lanes], stacked(k_ref[:, lanes], m0, m1), NT)
        hi, lo = halves(score * decay_pair(cumulative_t, cum_ref, p, row >= col, 1.0))
        both = stacked(v_ref[:, lanes], m0, m1)
        inside_ref[:, lanes] = mm(hi, both) + mm(lo, both)
        emit(p)


def middle_kernel(
    ready, emit, gain_ref, grow_ref, q_ref, g_ref, state_ref, inside_ref, stats_ref, out_ref, att
):
    length, features = q_ref.shape
    pairs = features // LANES
    m0, m1 = side(LANES)
    square = dot = jnp.zeros((length, LANES), F32)
    ready("gain")
    ready("grow")
    grow = grow_ref[...]
    for p in range(pairs):
        ready(p)
        lanes = pair(p)
        carried = carry(q_ref[:, lanes], *block_diagonal(state_ref[64 * p : 64 * p + 64], m0, m1))
        attended = inside_ref[:, lanes] + columns(grow, p) * carried
        att[:, lanes] = attended
        square = square + attended * attended
        dot = dot + attended * (gain_ref[:, lanes] * g_ref[:, lanes].astype(F32))
    scale = jnp.sqrt(jnp.sum(square, 1, keepdims=True) / features + EPSILON)
    inverse = 1.0 / scale
    slope = jnp.sum(dot, 1, keepdims=True) * (inverse * inverse * inverse) / features
    stats_ref[...] = jnp.where(iota(stats_ref.shape, 1) == 0, inverse, slope)
    for p in range(pairs):
        lanes = pair(p)
        attended = att[:, lanes]
        g = g_ref[:, lanes].astype(F32) * inverse
        gain_row = jnp.sum(g * attended, 0, keepdims=True)
        x = gain_ref[:, lanes] * g - attended * slope
        hi, lo = halves(columns(grow, p) * x)
        q_t = q_ref[:, lanes].T
        state = compact(mm(jnp.concatenate([q_t, q_t], 1), jnp.concatenate([hi, lo], 0)))
        send_state(out_ref, p, state, gain_row)
        emit(p)


def local_kernel(
    ready, emit, cum_ref, cum_t_ref, grow_ref, stats_ref, gain_ref,
    q_ref, k_ref, v_ref, g_ref, state_ref, inside_ref,
    z_ref, dq_ref, dk_ref, dv_ref,
):
    length, features = q_ref.shape
    heads = cum_ref.shape[0]
    m0, m1 = side(LANES)
    row, col = iota((length, length), 0), iota((length, length), 1)
    z = jnp.zeros((heads, length), F32)
    for name in ("cum", "cum_t", "grow", "stats", "gain"):
        ready(name)
    cum_t, grow = cum_t_ref[...], grow_ref[...]
    inverse, slope = stats_ref[:, 0:1], stats_ref[:, 1:2]
    for p in range(features // LANES):
        ready(p)
        lanes = pair(p)
        q, k, v = q_ref[:, lanes], k_ref[:, lanes], v_ref[:, lanes]
        state_hi, state_lo = block_diagonal(state_ref[64 * p : 64 * p + 64], m0, m1)
        growth = columns(grow, p)
        attended = inside_ref[:, lanes] + growth * carry(q, state_hi, state_lo)
        g = g_ref[:, lanes].astype(F32) * inverse
        x = gain_ref[:, lanes] * g - attended * slope
        x_hi, x_lo = halves(x)
        y_hi, y_lo = halves(growth * x)
        k2, q2, v2 = stacked(k, m0, m1), stacked(q, m0, m1), stacked(v, m0, m1)
        x2_hi, x2_lo = stacked(x_hi, m0, m1), stacked(x_lo, m0, m1)
        d_weight = mm(jnp.concatenate([x_hi, x_lo], 1), jnp.concatenate([v2, v2], 1), NT)
        hi, lo = halves(d_weight * decay_pair(cum_t, cum_ref, p, row >= col, 1.0))
        dq = mm(hi, k2) + mm(lo, k2) + mm(y_hi, state_lo, NT)
        dq = dq + mm(jnp.concatenate([y_hi, y_lo], 1), jnp.concatenate([state_hi, state_hi], 1), NT)
        dq_ref[:, lanes] = dq.astype(BF16)
        decay = decay_pair(cum_t, cum_ref, p, row <= col, -1.0)
        hi, lo = halves(mm(k, q2, NT) * decay)
        dv_ref[:, lanes] = mm(hi, x2_hi) + mm(lo, x2_hi) + mm(hi, x2_lo)
        d_weight = mm(jnp.concatenate([v, v], 1), jnp.concatenate([x2_hi, x2_lo], 1), NT)
        hi, lo = halves(d_weight * decay)
        dk = mm(hi, q2) + mm(lo, q2)
        dk_ref[:, lanes] = dk
        hi, lo = halves(q.astype(F32) * dq - k.astype(F32) * dk)
        z = z + mm(picker(heads, p), jnp.concatenate([hi, lo], 1), NT)
        emit(p)
    z_ref[...] = exact(z, (row >= col).astype(F32))


def picker(heads, p):
    lane = iota((heads, 2 * LANES), 1) & (LANES - 1)
    head = 2 * p + lane // 64
    return (iota((heads, 2 * LANES), 0) == head).astype(F32).astype(BF16)


def last_kernel(
    ready, emit, log_ref, z_ref, weight_ref, in_ref, k_ref, v_ref, state_ref, dk_in, dv_in,
    log_out, dk_ref, dv_ref, kept,
):
    length, features = k_ref.shape
    heads = log_ref.shape[0]
    m0, m1 = side(LANES)
    lane = iota((1, LANES), 1)
    u = jnp.zeros((heads, length), F32)
    ready("log")
    ready("z")
    ready("w")
    weight = weight_ref[...]
    for p in range(features // LANES):
        ready(p)
        lanes = pair(p)
        k, v, w = k_ref[:, lanes], v_ref[:, lanes], columns(weight, p)
        j = 17 * 4 * p
        grad = jnp.concatenate([in_ref[j + 17 * i : j + 17 * i + 16] for i in range(4)], 0)
        hi, lo = block_diagonal(grad, m0, m1)
        dk = w * mm(jnp.concatenate([v, v], 1), jnp.concatenate([hi, lo], 1), NT)
        dv = w * mm(jnp.concatenate([k, k], 1), jnp.concatenate([hi, lo], 0))
        dk_ref[:, lanes] = (dk_in[:, lanes] + dk).astype(BF16)
        dv_ref[:, lanes] = (dv_in[:, lanes] + dv).astype(BF16)
        part = jnp.sum(grad * state_ref[64 * p : 64 * p + 64], 0, keepdims=True)
        kept[2 * p : 2 * p + 1] = jnp.where(lane < 64, part, 0.0)
        kept[2 * p + 1 : 2 * p + 2] = jnp.where(lane < 64, 0.0, part)
        hi, lo = halves(k.astype(F32) * dk)
        u = u + mm(picker(heads, p), jnp.concatenate([hi, lo], 1), NT)
        emit(p)
    row, col = iota((length, length), 0), iota((length, length), 1)
    whole = jnp.exp(jnp.sum(log_ref[...], 1, keepdims=True)) * jnp.sum(kept[...], 1, keepdims=True)
    log_out[...] = z_ref[...] + exact(u, (row < col).astype(F32)) + whole


def call(kernel, outs, flops, *args):
    vmem = pl.BlockSpec(memory_space=pltpu.VMEM)
    outs = [jax.ShapeDtypeStruct(shape, dtype) for shape, dtype in outs]
    size = sum(a.size * a.dtype.itemsize for a in [*args, *outs])
    return pl.pallas_call(
        kernel,
        out_shape=outs,
        in_specs=[vmem] * len(args),
        out_specs=[vmem] * len(outs),
        cost_estimate=pl.CostEstimate(flops=flops, bytes_accessed=size, transcendentals=0),
        compiler_params=pltpu.CompilerParams(vmem_limit_bytes=4 << 20),
    )(*args)


def staged(kernel, flops, limit, pieces, ins, outs, scratch=()):
    in_shapes = [(a.shape, a.dtype) for a in ins.values()]
    out_shapes = list(outs.values())
    names = [*ins, *outs]
    shapes = in_shapes + out_shapes
    small = [math.prod(shape) <= 4096 for shape, _ in shapes]
    count = len(shapes)

    def body(*refs):
        far, near = refs[:count], refs[count : 2 * count]
        sems, own = refs[2 * count], refs[2 * count + 1 :]

        def copy(i, c):
            rows, lanes = shapes[i][0]
            cut = pieces[i >= len(ins)]
            if small[i]:
                a, b = far[i], near[i]
            elif lanes == LANES:
                part = pl.ds(c * (rows // cut), rows // cut)
                a, b = far[i].at[part, :], near[i].at[part, :]
            else:
                part = pl.ds(c * (lanes // cut), lanes // cut)
                a, b = far[i].at[:, part], near[i].at[:, part]
            if i >= len(ins):
                a, b = b, a
            return pltpu.make_async_copy(a, b, sems.at[i, c])

        came = range(len(ins))
        sent = range(len(ins), count)
        steps = [PAIRS // cut for cut in pieces]
        for i in came:
            if small[i]:
                copy(i, 0).start()
        for c in range(pieces[0]):
            for i in came:
                if not small[i]:
                    copy(i, c).start()

        def ready(p):
            for i in came:
                if small[i] and names[i] == p:
                    copy(i, 0).wait()
                if not small[i] and p in range(0, PAIRS, steps[0]):
                    copy(i, p // steps[0]).wait()

        def emit(p):
            for i in sent:
                if not small[i] and p % steps[1] == steps[1] - 1:
                    copy(i, p // steps[1]).start()

        kernel(ready, emit, *near, *own)
        for i in sent:
            if small[i]:
                copy(i, 0).start()
        for i in sent:
            for c in range(1 if small[i] else pieces[1]):
                copy(i, c).wait()

    hbm = pl.BlockSpec(memory_space=pltpu.HBM)
    results = [jax.ShapeDtypeStruct(shape, dtype) for shape, dtype in out_shapes]
    size = sum(math.prod(shape) * jnp.dtype(dtype).itemsize for shape, dtype in shapes)
    return pl.pallas_call(
        body,
        out_shape=results,
        in_specs=[hbm] * len(ins),
        out_specs=[hbm] * len(outs),
        scratch_shapes=[
            *(pltpu.VMEM(shape, dtype) for shape, dtype in shapes),
            pltpu.SemaphoreType.DMA((count, max(pieces))),
            *(pltpu.VMEM(shape, dtype) for shape, dtype in scratch),
        ],
        cost_estimate=pl.CostEstimate(flops=flops, bytes_accessed=size, transcendentals=0),
        compiler_params=pltpu.CompilerParams(vmem_limit_bytes=limit << 20),
    )(*ins.values())


def exchange(array, axis):
    count = lax.axis_size(axis)
    rows, lanes = array.shape
    pieces = array.reshape(count, 1, rows // count * lanes)
    return lax.all_to_all(pieces, axis, 0, 0, tiled=True).reshape(rows, lanes)


def shards(queries, keys, values, log_decay, gain, d_out):
    length, features = queries.shape[1:]
    heads = log_decay.shape[1]
    pairs = features // LANES
    count = lax.axis_size("seq")
    assert features == 32 * count and features == 64 * heads and length == LANES and pairs == PAIRS
    q, k, v, g, log = queries[0], keys[0], values[0], d_out[0], log_decay[0]
    wide = ((length, features), F32)
    half = ((length, features), BF16)
    small = ((heads, length), F32)
    turned = ((length, heads), F32)
    sent = ((17 * count, LANES), F32)

    (fresh,) = staged(fresh_kernel, 1 << 27, 60, (1, 2), dict(log=log, k=k, v=v), dict(out=sent))
    arrived = exchange(fresh, "seq")
    cum, cum_t, grow, weight, inside = staged(
        inside_kernel, 1 << 30, 60, (2, 2), dict(log=log, q=q, k=k, v=v),
        dict(cum=small, cum_t=turned, grow=turned, weight=turned, inside=wide),
    )
    arrived, inside = lax.optimization_barrier((arrived, inside))
    begun, decays = call(
        scan_kernel, [((16 * count, LANES), F32), ((count, LANES), F32)], 1 << 20, arrived
    )
    start = exchange(begun, "seq")
    stats, incoming = staged(
        middle_kernel, 1 << 28, 60, (2, 2),
        dict(gain=gain[None], grow=grow, q=q, g=g, state=start, inside=inside),
        dict(stats=turned, out=sent), [wide],
    )
    returned = exchange(incoming, "seq")
    z, d_queries, dk, dv = staged(
        local_kernel, 1 << 31, 60, (2, 2),
        dict(
            cum=cum, cum_t=cum_t, grow=grow, stats=stats, gain=gain[None],
            q=q, k=k, v=v, g=g, state=start, inside=inside,
        ),
        dict(z=small, dq=half, dk=wide, dv=wide),
    )
    returned, dk = lax.optimization_barrier((returned, dk))
    (ended,) = call(back_kernel, [sent], 1 << 20, returned, decays)
    ended = exchange(ended, "seq")
    shares = jax.ShapeDtypeStruct((lax.axis_size("dp"), pairs, LANES), F32)
    share = pl.pallas_call(
        gain_kernel,
        out_shape=shares,
        in_specs=[pl.BlockSpec(memory_space=pltpu.HBM)],
        out_specs=pl.BlockSpec(memory_space=pltpu.VMEM),
        scratch_shapes=[pltpu.VMEM((pairs, LANES), F32), pltpu.SemaphoreType.DMA((pairs,))],
        compiler_params=pltpu.CompilerParams(vmem_limit_bytes=60 << 20),
    )(ended)
    share = lax.all_to_all(share, "dp", 0, 0, tiled=True)
    (d_gain,) = call(gain_sum_kernel, [((pairs, LANES), F32)], 1 << 10, share)
    d_log, d_keys, d_values = staged(
        last_kernel, 1 << 28, 60, (2, 2),
        {"log": log, "z": z, "w": weight, "in": ended, "k": k, "v": v, "s": start, "dk": dk, "dv": dv},
        dict(log=small, dk=half, dv=half), [((heads, LANES), F32)],
    )
    return d_queries[None], d_keys[None], d_values[None], d_log[None], d_gain.reshape(features)


def solution(mesh):
    tokens, decays = P("dp", "seq", None), P("dp", None, "seq")
    return jax.shard_map(
        shards,
        mesh=mesh,
        in_specs=(tokens, tokens, tokens, decays, P(), tokens),
        out_specs=(tokens, tokens, tokens, decays, P()),
        check_vma=False,
    )
```

```python
import math

import jax
import jax.numpy as jnp
from jax import lax
from jax.experimental import pallas as pl
from jax.experimental.pallas import tpu as pltpu
from jax.sharding import PartitionSpec as P

HIGH = lax.Precision.HIGHEST
EPSILON = 1e-06
F32 = jnp.float32
BF16 = jnp.bfloat16
LANES = 128
PAIRS = 16
NN = (((1,), (0,)), ((), ()))
NT = (((1,), (1,)), ((), ()))
TN = (((0,), (0,)), ((), ()))


def mm(a, b, dims=NN):
    return lax.dot_general(a, b, dims, preferred_element_type=F32)


def exact(a, b, dims=NN):
    return lax.dot_general(a, b, dims, precision=HIGH, preferred_element_type=F32)


def iota(shape, axis):
    return lax.broadcasted_iota(jnp.int32, shape, axis)


def halves(x):
    hi = x.astype(BF16)
    return hi, (x - hi.astype(F32)).astype(BF16)


def columns(x, p):
    lane = iota((1, LANES), 1)
    return jnp.where(lane < LANES // 2, x[:, 2 * p : 2 * p + 1], x[:, 2 * p + 1 : 2 * p + 2])


def side(width):
    lane = iota((1, width), 1) & (LANES - 1)
    first = jnp.where(lane < LANES // 2, 1.0, 0.0).astype(F32)
    return first.astype(BF16), (1.0 - first).astype(BF16)


def stacked(x, m0, m1):
    return jnp.concatenate([x * m0, x * m1], axis=0)


def compact(full):
    lane = iota((LANES // 2, LANES), 1)
    return jnp.where(lane < LANES // 2, full[: LANES // 2], full[LANES // 2 :])


def sums(log, length):
    row, col = iota((length, length), 0), iota((length, length), 1)
    cumulative_t = exact((col <= row).astype(F32), log, NT)
    return cumulative_t, cumulative_t[length - 1 : length]


def pair(p):
    return slice(p * LANES, (p + 1) * LANES)


def block_diagonal(state, m0, m1):
    hi, lo = halves(state)
    return stacked(hi, m0, m1), stacked(lo, m0, m1)


def carry(q, state_hi, state_lo):
    return mm(jnp.concatenate([q, q], 1), jnp.concatenate([state_hi, state_lo], 0))


def decay_pair(cum_t, cum_ref, p, keep, sign):
    parts = []
    for h in (2 * p, 2 * p + 1):
        spread = cum_t[:, h : h + 1] - cum_ref[h : h + 1, :]
        parts.append(jnp.where(keep, jnp.exp(jnp.minimum(sign * spread, 0.0)), 0.0))
    return jnp.concatenate(parts, 1)


def send_state(out_ref, p, state, row):
    for i in range(4):
        j = 17 * (4 * p + i)
        out_ref[j : j + 16] = state[16 * i : 16 * i + 16]
        out_ref[j + 16 : j + 17] = row


def fresh_kernel(ready, emit, log_ref, k_ref, v_ref, out_ref):
    length, features = k_ref.shape
    ready("log")
    cumulative_t, total = sums(log_ref[...], length)
    weight, ends = jnp.exp(total - cumulative_t), jnp.exp(total)
    for p in range(features // LANES):
        ready(p)
        lanes = pair(p)
        k_t = k_ref[:, lanes].T
        hi, lo = halves(columns(weight, p) * v_ref[:, lanes].astype(F32))
        state = compact(mm(jnp.concatenate([k_t, k_t], 1), jnp.concatenate([hi, lo], 0)))
        send_state(out_ref, p, state, columns(ends, p))
        emit(p)


def scan_kernel(in_ref, out_ref, decay_ref):
    count = decay_ref.shape[0]
    state = jnp.zeros((16, LANES), F32)
    for m in range(count):
        out_ref[16 * m : 16 * m + 16] = state
        decay = in_ref[17 * m + 16 : 17 * m + 17]
        decay_ref[m : m + 1] = decay
        state = decay * state + in_ref[17 * m : 17 * m + 16]


def back_kernel(in_ref, decay_ref, out_ref):
    count = decay_ref.shape[0]
    gain = in_ref[16:17]
    for m in range(1, count):
        gain = gain + in_ref[17 * m + 16 : 17 * m + 17]
    state = jnp.zeros((16, LANES), F32)
    for m in range(count - 1, -1, -1):
        out_ref[17 * m : 17 * m + 16] = state
        out_ref[17 * m + 16 : 17 * m + 17] = gain
        state = decay_ref[m : m + 1] * state + in_ref[17 * m : 17 * m + 16]


def gain_kernel(in_ref, out_ref):
    pairs = out_ref.shape[1]
    for p in range(pairs):
        row = in_ref[17 * 4 * p + 16 : 17 * 4 * p + 17]
        for d in range(out_ref.shape[0]):
            out_ref[d, p : p + 1] = row


def gain_sum_kernel(in_ref, out_ref):
    total = in_ref[0]
    for d in range(1, in_ref.shape[0]):
        total = total + in_ref[d]
    out_ref[...] = total


def inside_kernel(
    ready, emit, log_ref, q_ref, k_ref, v_ref, cum_ref, cum_t_ref, weight_ref, inside_ref
):
    length, features = q_ref.shape
    ready("log")
    log = log_ref[...]
    row, col = iota((length, length), 0), iota((length, length), 1)
    cum_ref[...] = exact(log, (row <= col).astype(F32))
    cumulative_t, total = sums(log, length)
    cum_t_ref[...] = cumulative_t
    inside_ref[:, features : features + log.shape[0]] = jnp.exp(cumulative_t)
    inside_ref[:, features + log.shape[0] :] = jnp.zeros((length, LANES - log.shape[0]), F32)
    weight_ref[...] = jnp.exp(total - cumulative_t)
    m0, m1 = side(LANES)
    for p in range(features // LANES):
        ready(p)
        lanes = pair(p)
        score = mm(q_ref[:, lanes], stacked(k_ref[:, lanes], m0, m1), NT)
        hi, lo = halves(score * decay_pair(cumulative_t, cum_ref, p, row >= col, 1.0))
        both = stacked(v_ref[:, lanes], m0, m1)
        inside_ref[:, lanes] = mm(hi, both) + mm(lo, both)
        emit(p)


def growth_of(inside_ref, features):
    return inside_ref[:, features : features + features // 64]


def attend(ready, gain_ref, grow, q_ref, g_ref, state_ref, inside_ref, att):
    length, features = q_ref.shape
    m0, m1 = side(LANES)
    square = dot = jnp.zeros((length, LANES), F32)
    for p in range(features // LANES):
        ready(p)
        lanes = pair(p)
        state = block_diagonal(state_ref[64 * p : 64 * p + 64], m0, m1)
        attended = inside_ref[:, lanes] + columns(grow, p) * carry(q_ref[:, lanes], *state)
        att[:, lanes] = attended
        square = square + attended * attended
        dot = dot + attended * (gain_ref[:, lanes] * g_ref[:, lanes].astype(F32))
    scale = jnp.sqrt(jnp.sum(square, 1, keepdims=True) / features + EPSILON)
    inverse = 1.0 / scale
    return inverse, jnp.sum(dot, 1, keepdims=True) * (inverse * inverse * inverse) / features


def middle_kernel(
    ready, emit, gain_ref, q_ref, g_ref, state_ref, inside_ref, out_ref, att
):
    features = q_ref.shape[1]
    grow = growth_of(inside_ref, features)
    inverse, slope = attend(ready, gain_ref, grow, q_ref, g_ref, state_ref, inside_ref, att)
    for p in range(features // LANES):
        lanes = pair(p)
        attended = att[:, lanes]
        g = g_ref[:, lanes].astype(F32) * inverse
        gain_row = jnp.sum(g * attended, 0, keepdims=True)
        x = gain_ref[:, lanes] * g - attended * slope
        hi, lo = halves(columns(grow, p) * x)
        q_t = q_ref[:, lanes].T
        state = compact(mm(jnp.concatenate([q_t, q_t], 1), jnp.concatenate([hi, lo], 0)))
        send_state(out_ref, p, state, gain_row)
        emit(p)


def local_kernel(
    ready, emit, cum_ref, cum_t_ref, gain_ref, q_ref, k_ref, v_ref, g_ref, state_ref, inside_ref,
    z_ref, dq_ref, dk_ref, dv_ref, att,
):
    length, features = q_ref.shape
    heads = cum_ref.shape[0]
    m0, m1 = side(LANES)
    row, col = iota((length, length), 0), iota((length, length), 1)
    z = jnp.zeros((heads, length), F32)
    for name in ("cum", "cum_t", "gain", 0):
        ready(name)
    cum_t, grow = cum_t_ref[...], growth_of(inside_ref, features)
    inverse, slope = attend(
        lambda p: None, gain_ref, grow, q_ref, g_ref, state_ref, inside_ref, att
    )
    for p in range(features // LANES):
        lanes = pair(p)
        q, k, v = q_ref[:, lanes], k_ref[:, lanes], v_ref[:, lanes]
        state_hi, state_lo = block_diagonal(state_ref[64 * p : 64 * p + 64], m0, m1)
        growth = columns(grow, p)
        attended = att[:, lanes]
        g = g_ref[:, lanes].astype(F32) * inverse
        x = gain_ref[:, lanes] * g - attended * slope
        x_hi, x_lo = halves(x)
        y_hi, y_lo = halves(growth * x)
        k2, q2, v2 = stacked(k, m0, m1), stacked(q, m0, m1), stacked(v, m0, m1)
        x2_hi, x2_lo = stacked(x_hi, m0, m1), stacked(x_lo, m0, m1)
        d_weight = mm(jnp.concatenate([x_hi, x_lo], 1), jnp.concatenate([v2, v2], 1), NT)
        hi, lo = halves(d_weight * decay_pair(cum_t, cum_ref, p, row >= col, 1.0))
        dq = mm(hi, k2) + mm(lo, k2) + mm(y_hi, state_lo, NT)
        dq = dq + mm(jnp.concatenate([y_hi, y_lo], 1), jnp.concatenate([state_hi, state_hi], 1), NT)
        dq_ref[:, lanes] = dq.astype(BF16)
        decay = decay_pair(cum_t, cum_ref, p, row <= col, -1.0)
        hi, lo = halves(mm(k, q2, NT) * decay)
        dv_ref[:, lanes] = mm(hi, x2_hi) + mm(lo, x2_hi) + mm(hi, x2_lo)
        d_weight = mm(jnp.concatenate([v, v], 1), jnp.concatenate([x2_hi, x2_lo], 1), NT)
        hi, lo = halves(d_weight * decay)
        dk = mm(hi, q2) + mm(lo, q2)
        dk_ref[:, lanes] = dk
        hi, lo = halves(q.astype(F32) * dq - k.astype(F32) * dk)
        z = z + mm(picker(heads, p), jnp.concatenate([hi, lo], 1), NT)
        emit(p)
    z_ref[...] = exact(z, (row >= col).astype(F32))


def picker(heads, p):
    lane = iota((heads, 2 * LANES), 1) & (LANES - 1)
    head = 2 * p + lane // 64
    return (iota((heads, 2 * LANES), 0) == head).astype(F32).astype(BF16)


def last_kernel(
    ready, emit, log_ref, z_ref, weight_ref, in_ref, k_ref, v_ref, state_ref, dk_in, dv_in,
    log_out, dk_ref, dv_ref, kept,
):
    length, features = k_ref.shape
    heads = log_ref.shape[0]
    m0, m1 = side(LANES)
    lane = iota((1, LANES), 1)
    u = jnp.zeros((heads, length), F32)
    ready("log")
    ready("z")
    ready("w")
    weight = weight_ref[...]
    for p in range(features // LANES):
        ready(p)
        lanes = pair(p)
        k, v, w = k_ref[:, lanes], v_ref[:, lanes], columns(weight, p)
        j = 17 * 4 * p
        grad = jnp.concatenate([in_ref[j + 17 * i : j + 17 * i + 16] for i in range(4)], 0)
        hi, lo = block_diagonal(grad, m0, m1)
        dk = w * mm(jnp.concatenate([v, v], 1), jnp.concatenate([hi, lo], 1), NT)
        dv = w * mm(jnp.concatenate([k, k], 1), jnp.concatenate([hi, lo], 0))
        dk_ref[:, lanes] = (dk_in[:, lanes] + dk).astype(BF16)
        dv_ref[:, lanes] = (dv_in[:, lanes] + dv).astype(BF16)
        part = jnp.sum(grad * state_ref[64 * p : 64 * p + 64], 0, keepdims=True)
        kept[2 * p : 2 * p + 1] = jnp.where(lane < 64, part, 0.0)
        kept[2 * p + 1 : 2 * p + 2] = jnp.where(lane < 64, 0.0, part)
        hi, lo = halves(k.astype(F32) * dk)
        u = u + mm(picker(heads, p), jnp.concatenate([hi, lo], 1), NT)
        emit(p)
    row, col = iota((length, length), 0), iota((length, length), 1)
    whole = jnp.exp(jnp.sum(log_ref[...], 1, keepdims=True)) * jnp.sum(kept[...], 1, keepdims=True)
    log_out[...] = z_ref[...] + exact(u, (row < col).astype(F32)) + whole


def call(kernel, outs, flops, *args):
    vmem = pl.BlockSpec(memory_space=pltpu.VMEM)
    outs = [jax.ShapeDtypeStruct(shape, dtype) for shape, dtype in outs]
    size = sum(a.size * a.dtype.itemsize for a in [*args, *outs])
    return pl.pallas_call(
        kernel,
        out_shape=outs,
        in_specs=[vmem] * len(args),
        out_specs=[vmem] * len(outs),
        cost_estimate=pl.CostEstimate(flops=flops, bytes_accessed=size, transcendentals=0),
        compiler_params=pltpu.CompilerParams(vmem_limit_bytes=4 << 20),
    )(*args)


def staged(kernel, flops, limit, pieces, ins, outs, scratch=(), close=False):
    in_shapes = [(a.shape, a.dtype) for a in ins.values()]
    out_shapes = list(outs.values())
    names = [*ins, *outs]
    shapes = in_shapes + out_shapes
    small = [math.prod(shape) <= 4096 for shape, _ in shapes]
    count = len(shapes)
    first = len(ins) if close else 0

    def body(*refs):
        far, near = refs[:count], refs[:first] + refs[count : 2 * count - first]
        sems, own = refs[2 * count - first], refs[2 * count - first + 1 :]

        def copy(i, c):
            rows, lanes = shapes[i][0]
            cut = pieces[i >= len(ins)]
            if small[i]:
                a, b = far[i], near[i]
            elif lanes == LANES:
                part = pl.ds(c * (rows // cut), rows // cut)
                a, b = far[i].at[part, :], near[i].at[part, :]
            else:
                part = pl.ds(c * (lanes // cut), lanes // cut)
                a, b = far[i].at[:, part], near[i].at[:, part]
            if i >= len(ins):
                a, b = b, a
            return pltpu.make_async_copy(a, b, sems.at[i, c])

        came = range(first, len(ins))
        sent = range(len(ins), count)
        steps = [PAIRS // cut for cut in pieces]
        for i in came:
            if small[i]:
                copy(i, 0).start()
        for c in range(pieces[0]):
            for i in came:
                if not small[i]:
                    copy(i, c).start()

        def ready(p):
            for i in came:
                if small[i] and names[i] == p:
                    copy(i, 0).wait()
                if not small[i] and p in range(0, PAIRS, steps[0]):
                    copy(i, p // steps[0]).wait()

        def emit(p):
            for i in sent:
                if not small[i] and p % steps[1] == steps[1] - 1:
                    copy(i, p // steps[1]).start()

        kernel(ready, emit, *near, *own)
        for i in sent:
            if small[i]:
                copy(i, 0).start()
        for i in sent:
            for c in range(1 if small[i] else pieces[1]):
                copy(i, c).wait()

    hbm = pl.BlockSpec(memory_space=pltpu.HBM)
    results = [jax.ShapeDtypeStruct(shape, dtype) for shape, dtype in out_shapes]
    size = sum(math.prod(shape) * jnp.dtype(dtype).itemsize for shape, dtype in shapes)
    return pl.pallas_call(
        body,
        out_shape=results,
        in_specs=[pl.BlockSpec(memory_space=pltpu.VMEM) if close else hbm] * len(ins),
        out_specs=[hbm] * len(outs),
        scratch_shapes=[
            *(pltpu.VMEM(shape, dtype) for shape, dtype in shapes[first:]),
            pltpu.SemaphoreType.DMA((count, max(pieces))),
            *(pltpu.VMEM(shape, dtype) for shape, dtype in scratch),
        ],
        cost_estimate=pl.CostEstimate(flops=flops, bytes_accessed=size, transcendentals=0),
        compiler_params=pltpu.CompilerParams(vmem_limit_bytes=limit << 20),
    )(*ins.values())


def exchange(array, axis):
    count = lax.axis_size(axis)
    rows, lanes = array.shape
    pieces = array.reshape(count, 1, rows // count * lanes)
    return lax.all_to_all(pieces, axis, 0, 0, tiled=True).reshape(rows, lanes)


def shards(queries, keys, values, log_decay, gain, d_out):
    length, features = queries.shape[1:]
    heads = log_decay.shape[1]
    pairs = features // LANES
    count = lax.axis_size("seq")
    assert features == 32 * count and features == 64 * heads and length == LANES and pairs == PAIRS
    q, k, v, g, log = queries[0], keys[0], values[0], d_out[0], log_decay[0]
    wide = ((length, features), F32)
    half = ((length, features), BF16)
    small = ((heads, length), F32)
    turned = ((length, heads), F32)
    sent = ((17 * count, LANES), F32)

    (fresh,) = staged(fresh_kernel, 1 << 27, 60, (1, 2), dict(log=log, k=k, v=v), dict(out=sent))
    arrived = exchange(fresh, "seq")
    cum, cum_t, weight, inside = staged(
        inside_kernel, 1 << 30, 60, (2, 1), dict(log=log, q=q, k=k, v=v),
        dict(cum=small, cum_t=turned, weight=turned, inside=((length, features + LANES), F32)),
    )
    arrived, inside = lax.optimization_barrier((arrived, inside))
    begun, decays = call(
        scan_kernel, [((16 * count, LANES), F32), ((count, LANES), F32)], 1 << 20, arrived
    )
    start = exchange(begun, "seq")
    (incoming,) = staged(
        middle_kernel, 1 << 28, 8, (1, 2),
        dict(gain=gain[None], q=q, g=g, state=start, inside=inside),
        dict(out=sent), [wide], close=True,
    )
    returned = exchange(incoming, "seq")
    z, d_queries, dk, dv = staged(
        local_kernel, 1 << 31, 60, (1, 2),
        dict(
            cum=cum, cum_t=cum_t, gain=gain[None],
            q=q, k=k, v=v, g=g, state=start, inside=inside,
        ),
        dict(z=small, dq=half, dk=wide, dv=wide), [wide],
    )
    returned, dk = lax.optimization_barrier((returned, dk))
    (ended,) = call(back_kernel, [sent], 1 << 20, returned, decays)
    ended = exchange(ended, "seq")
    shares = ((lax.axis_size("dp"), pairs, LANES), F32)
    (share,) = call(gain_kernel, [shares], 1 << 10, ended)
    share = lax.all_to_all(share, "dp", 0, 0, tiled=True)
    (d_gain,) = call(gain_sum_kernel, [((pairs, LANES), F32)], 1 << 10, share)
    d_log, d_keys, d_values = staged(
        last_kernel, 1 << 28, 60, (2, 2),
        {"log": log, "z": z, "w": weight, "in": ended, "k": k, "v": v, "s": start, "dk": dk, "dv": dv},
        dict(log=small, dk=half, dv=half), [((heads, LANES), F32)],
    )
    return d_queries[None], d_keys[None], d_values[None], d_log[None], d_gain.reshape(features)


def solution(mesh):
    tokens, decays = P("dp", "seq", None), P("dp", None, "seq")
    return jax.shard_map(
        shards,
        mesh=mesh,
        in_specs=(tokens, tokens, tokens, decays, P(), tokens),
        out_specs=(tokens, tokens, tokens, decays, P()),
        check_vma=False,
    )
```

```python
import math

import jax
import jax.numpy as jnp
from jax import lax
from jax.experimental import pallas as pl
from jax.experimental.pallas import tpu as pltpu
from jax.sharding import PartitionSpec as P

HIGH = lax.Precision.HIGHEST
EPSILON = 1e-06
F32 = jnp.float32
BF16 = jnp.bfloat16
LANES = 128
PAIRS = 16
NN = (((1,), (0,)), ((), ()))
NT = (((1,), (1,)), ((), ()))
TN = (((0,), (0,)), ((), ()))


def mm(a, b, dims=NN):
    return lax.dot_general(a, b, dims, preferred_element_type=F32)


def exact(a, b, dims=NN):
    return lax.dot_general(a, b, dims, precision=HIGH, preferred_element_type=F32)


def iota(shape, axis):
    return lax.broadcasted_iota(jnp.int32, shape, axis)


def halves(x):
    hi = x.astype(BF16)
    return hi, (x - hi.astype(F32)).astype(BF16)


def columns(x, p):
    lane = iota((1, LANES), 1)
    return jnp.where(lane < LANES // 2, x[:, 2 * p : 2 * p + 1], x[:, 2 * p + 1 : 2 * p + 2])


def side(width):
    lane = iota((1, width), 1) & (LANES - 1)
    first = jnp.where(lane < LANES // 2, 1.0, 0.0).astype(F32)
    return first.astype(BF16), (1.0 - first).astype(BF16)


def stacked(x, m0, m1):
    return jnp.concatenate([x * m0, x * m1], axis=0)


def compact(full):
    lane = iota((LANES // 2, LANES), 1)
    return jnp.where(lane < LANES // 2, full[: LANES // 2], full[LANES // 2 :])


def sums(log, length):
    row, col = iota((length, length), 0), iota((length, length), 1)
    cumulative_t = exact((col <= row).astype(F32), log, NT)
    return cumulative_t, cumulative_t[length - 1 : length]


def pair(p):
    return slice(p * LANES, (p + 1) * LANES)


def block_diagonal(state, m0, m1):
    hi, lo = halves(state)
    return stacked(hi, m0, m1), stacked(lo, m0, m1)


def carry(q, state_hi, state_lo):
    return mm(jnp.concatenate([q, q], 1), jnp.concatenate([state_hi, state_lo], 0))


def decay_pair(cum_t, cum_ref, p, keep, sign):
    parts = []
    for h in (2 * p, 2 * p + 1):
        spread = cum_t[:, h : h + 1] - cum_ref[h : h + 1, :]
        parts.append(jnp.where(keep, jnp.exp(jnp.minimum(sign * spread, 0.0)), 0.0))
    return jnp.concatenate(parts, 1)


def send_state(out_ref, p, state, row):
    for i in range(4):
        j = 17 * (4 * p + i)
        out_ref[j : j + 16] = state[16 * i : 16 * i + 16]
        out_ref[j + 16 : j + 17] = row


def tied(product, moves_t, moves, p, keep):
    parts = []
    for a in range(2):
        h = 2 * p + a
        same = keep & (moves_t[:, h : h + 1] == moves[h : h + 1, :])
        parts.append(jnp.sum(jnp.where(same, product[:, pair(a)], 0.0), 0, keepdims=True))
    return jnp.concatenate(parts, 1)


def fresh_kernel(ready, emit, log_ref, k_ref, v_ref, out_ref):
    length, features = k_ref.shape
    ready("log")
    cumulative_t, total = sums(log_ref[...], length)
    weight, ends = jnp.exp(total - cumulative_t), jnp.exp(total)
    for p in range(features // LANES):
        ready(p)
        lanes = pair(p)
        k_t = k_ref[:, lanes].T
        hi, lo = halves(columns(weight, p) * v_ref[:, lanes].astype(F32))
        state = compact(mm(jnp.concatenate([k_t, k_t], 1), jnp.concatenate([hi, lo], 0)))
        send_state(out_ref, p, state, columns(ends, p))
        emit(p)


def scan_kernel(in_ref, out_ref, decay_ref):
    count = decay_ref.shape[0]
    state = jnp.zeros((16, LANES), F32)
    for m in range(count):
        out_ref[16 * m : 16 * m + 16] = state
        decay = in_ref[17 * m + 16 : 17 * m + 17]
        decay_ref[m : m + 1] = decay
        state = decay * state + in_ref[17 * m : 17 * m + 16]


def back_kernel(in_ref, decay_ref, out_ref):
    count = decay_ref.shape[0]
    gain = in_ref[16:17]
    for m in range(1, count):
        gain = gain + in_ref[17 * m + 16 : 17 * m + 17]
    state = jnp.zeros((16, LANES), F32)
    for m in range(count - 1, -1, -1):
        out_ref[17 * m : 17 * m + 16] = state
        out_ref[17 * m + 16 : 17 * m + 17] = gain
        state = decay_ref[m : m + 1] * state + in_ref[17 * m : 17 * m + 16]


def gain_kernel(in_ref, out_ref):
    pairs = out_ref.shape[1]
    for p in range(pairs):
        row = in_ref[17 * 4 * p + 16 : 17 * 4 * p + 17]
        for d in range(out_ref.shape[0]):
            out_ref[d, p : p + 1] = row


def gain_sum_kernel(in_ref, out_ref):
    total = in_ref[0]
    for d in range(1, in_ref.shape[0]):
        total = total + in_ref[d]
    out_ref[...] = total


def inside_kernel(
    ready, emit, log_ref, q_ref, k_ref, v_ref, cum_ref, cum_t_ref, weight_ref, inside_ref
):
    length, features = q_ref.shape
    ready("log")
    log = log_ref[...]
    row, col = iota((length, length), 0), iota((length, length), 1)
    cum_ref[...] = exact(log, (row <= col).astype(F32))
    cumulative_t, total = sums(log, length)
    cum_t_ref[...] = cumulative_t
    inside_ref[:, features : features + log.shape[0]] = jnp.exp(cumulative_t)
    inside_ref[:, features + log.shape[0] :] = jnp.zeros((length, LANES - log.shape[0]), F32)
    weight_ref[...] = jnp.exp(total - cumulative_t)
    m0, m1 = side(LANES)
    for p in range(features // LANES):
        ready(p)
        lanes = pair(p)
        score = mm(q_ref[:, lanes], stacked(k_ref[:, lanes], m0, m1), NT)
        hi, lo = halves(score * decay_pair(cumulative_t, cum_ref, p, row >= col, 1.0))
        both = stacked(v_ref[:, lanes], m0, m1)
        inside_ref[:, lanes] = mm(hi, both) + mm(lo, both)
        emit(p)


def growth_of(inside_ref, features):
    return inside_ref[:, features : features + features // 64]


def attend(ready, gain_ref, grow, q_ref, g_ref, state_ref, inside_ref, att):
    length, features = q_ref.shape
    m0, m1 = side(LANES)
    square = dot = jnp.zeros((length, LANES), F32)
    for p in range(features // LANES):
        ready(p)
        lanes = pair(p)
        state = block_diagonal(state_ref[64 * p : 64 * p + 64], m0, m1)
        attended = inside_ref[:, lanes] + columns(grow, p) * carry(q_ref[:, lanes], *state)
        att[:, lanes] = attended
        square = square + attended * attended
        dot = dot + attended * (gain_ref[:, lanes] * g_ref[:, lanes].astype(F32))
    scale = jnp.sqrt(jnp.sum(square, 1, keepdims=True) / features + EPSILON)
    inverse = 1.0 / scale
    return inverse, jnp.sum(dot, 1, keepdims=True) * (inverse * inverse * inverse) / features


def middle_kernel(
    ready, emit, gain_ref, q_ref, g_ref, state_ref, inside_ref, out_ref, att
):
    features = q_ref.shape[1]
    grow = growth_of(inside_ref, features)
    inverse, slope = attend(ready, gain_ref, grow, q_ref, g_ref, state_ref, inside_ref, att)
    for p in range(features // LANES):
        lanes = pair(p)
        attended = att[:, lanes]
        g = g_ref[:, lanes].astype(F32) * inverse
        gain_row = jnp.sum(g * attended, 0, keepdims=True)
        x = gain_ref[:, lanes] * g - attended * slope
        hi, lo = halves(columns(grow, p) * x)
        q_t = q_ref[:, lanes].T
        state = compact(mm(jnp.concatenate([q_t, q_t], 1), jnp.concatenate([hi, lo], 0)))
        send_state(out_ref, p, state, gain_row)
        emit(p)


def local_kernel(
    ready, emit, log_ref, cum_ref, cum_t_ref, gain_ref,
    q_ref, k_ref, v_ref, g_ref, state_ref, inside_ref,
    z_ref, dq_ref, dk_ref, dv_ref, att, ties,
):
    length, features = q_ref.shape
    heads = cum_ref.shape[0]
    m0, m1 = side(LANES)
    row, col = iota((length, length), 0), iota((length, length), 1)
    z = jnp.zeros((heads, length), F32)
    for name in ("log", "cum", "cum_t", "gain", 0):
        ready(name)
    cum_t, grow = cum_t_ref[...], growth_of(inside_ref, features)
    moved = (log_ref[...] != 0.0).astype(F32).astype(BF16)
    moves = mm(moved, (row <= col).astype(F32).astype(BF16))
    moves_t = mm((row >= col).astype(F32).astype(BF16), moved, NT)
    inverse, slope = attend(
        lambda p: None, gain_ref, grow, q_ref, g_ref, state_ref, inside_ref, att
    )
    for p in range(features // LANES):
        lanes = pair(p)
        q, k, v = q_ref[:, lanes], k_ref[:, lanes], v_ref[:, lanes]
        state_hi, state_lo = block_diagonal(state_ref[64 * p : 64 * p + 64], m0, m1)
        growth = columns(grow, p)
        attended = att[:, lanes]
        g = g_ref[:, lanes].astype(F32) * inverse
        x = gain_ref[:, lanes] * g - attended * slope
        x_hi, x_lo = halves(x)
        y_hi, y_lo = halves(growth * x)
        k2, q2, v2 = stacked(k, m0, m1), stacked(q, m0, m1), stacked(v, m0, m1)
        x2_hi, x2_lo = stacked(x_hi, m0, m1), stacked(x_lo, m0, m1)
        d_weight = mm(jnp.concatenate([x_hi, x_lo], 1), jnp.concatenate([v2, v2], 1), NT)
        d_score = d_weight * decay_pair(cum_t, cum_ref, p, row >= col, 1.0)
        down = tied(d_score * mm(q, k2, NT), moves_t, moves, p, row >= col)
        hi, lo = halves(d_score)
        dq = mm(hi, k2) + mm(lo, k2) + mm(y_hi, state_lo, NT)
        dq = dq + mm(jnp.concatenate([y_hi, y_lo], 1), jnp.concatenate([state_hi, state_hi], 1), NT)
        dq_ref[:, lanes] = dq.astype(BF16)
        decay = decay_pair(cum_t, cum_ref, p, row <= col, -1.0)
        score = mm(k, q2, NT)
        hi, lo = halves(score * decay)
        dv_ref[:, lanes] = mm(hi, x2_hi) + mm(lo, x2_hi) + mm(hi, x2_lo)
        d_weight = mm(jnp.concatenate([v, v], 1), jnp.concatenate([x2_hi, x2_lo], 1), NT)
        d_score = d_weight * decay
        across = tied(d_score * score, moves_t, moves, p, row <= col)
        for a in range(2):
            ties[2 * p + a : 2 * p + a + 1] = 0.5 * (down - across)[:, pair(a)]
        hi, lo = halves(d_score)
        dk = mm(hi, q2) + mm(lo, q2)
        dk_ref[:, lanes] = dk
        hi, lo = halves(q.astype(F32) * dq - k.astype(F32) * dk)
        z = z + mm(picker(heads, p), jnp.concatenate([hi, lo], 1), NT)
        emit(p)
    z_ref[...] = exact(z + ties[...], (row >= col).astype(F32))


def picker(heads, p):
    lane = iota((heads, 2 * LANES), 1) & (LANES - 1)
    head = 2 * p + lane // 64
    return (iota((heads, 2 * LANES), 0) == head).astype(F32).astype(BF16)


def last_kernel(
    ready, emit, log_ref, z_ref, weight_ref, in_ref, k_ref, v_ref, state_ref, dk_in, dv_in,
    log_out, dk_ref, dv_ref, kept,
):
    length, features = k_ref.shape
    heads = log_ref.shape[0]
    m0, m1 = side(LANES)
    lane = iota((1, LANES), 1)
    u = jnp.zeros((heads, length), F32)
    ready("log")
    ready("z")
    ready("w")
    weight = weight_ref[...]
    for p in range(features // LANES):
        ready(p)
        lanes = pair(p)
        k, v, w = k_ref[:, lanes], v_ref[:, lanes], columns(weight, p)
        j = 17 * 4 * p
        grad = jnp.concatenate([in_ref[j + 17 * i : j + 17 * i + 16] for i in range(4)], 0)
        hi, lo = block_diagonal(grad, m0, m1)
        dk = w * mm(jnp.concatenate([v, v], 1), jnp.concatenate([hi, lo], 1), NT)
        dv = w * mm(jnp.concatenate([k, k], 1), jnp.concatenate([hi, lo], 0))
        dk_ref[:, lanes] = (dk_in[:, lanes] + dk).astype(BF16)
        dv_ref[:, lanes] = (dv_in[:, lanes] + dv).astype(BF16)
        part = jnp.sum(grad * state_ref[64 * p : 64 * p + 64], 0, keepdims=True)
        kept[2 * p : 2 * p + 1] = jnp.where(lane < 64, part, 0.0)
        kept[2 * p + 1 : 2 * p + 2] = jnp.where(lane < 64, 0.0, part)
        hi, lo = halves(k.astype(F32) * dk)
        u = u + mm(picker(heads, p), jnp.concatenate([hi, lo], 1), NT)
        emit(p)
    row, col = iota((length, length), 0), iota((length, length), 1)
    whole = jnp.exp(jnp.sum(log_ref[...], 1, keepdims=True)) * jnp.sum(kept[...], 1, keepdims=True)
    log_out[...] = z_ref[...] + exact(u, (row < col).astype(F32)) + whole


def call(kernel, outs, flops, *args):
    vmem = pl.BlockSpec(memory_space=pltpu.VMEM)
    outs = [jax.ShapeDtypeStruct(shape, dtype) for shape, dtype in outs]
    size = sum(a.size * a.dtype.itemsize for a in [*args, *outs])
    return pl.pallas_call(
        kernel,
        out_shape=outs,
        in_specs=[vmem] * len(args),
        out_specs=[vmem] * len(outs),
        cost_estimate=pl.CostEstimate(flops=flops, bytes_accessed=size, transcendentals=0),
        compiler_params=pltpu.CompilerParams(vmem_limit_bytes=4 << 20),
    )(*args)


def staged(kernel, flops, limit, pieces, ins, outs, scratch=(), close=False):
    in_shapes = [(a.shape, a.dtype) for a in ins.values()]
    out_shapes = list(outs.values())
    names = [*ins, *outs]
    shapes = in_shapes + out_shapes
    small = [math.prod(shape) <= 4096 for shape, _ in shapes]
    count = len(shapes)
    first = len(ins) if close else 0

    def body(*refs):
        far, near = refs[:count], refs[:first] + refs[count : 2 * count - first]
        sems, own = refs[2 * count - first], refs[2 * count - first + 1 :]

        def copy(i, c):
            rows, lanes = shapes[i][0]
            cut = pieces[i >= len(ins)]
            if small[i]:
                a, b = far[i], near[i]
            elif lanes == LANES:
                part = pl.ds(c * (rows // cut), rows // cut)
                a, b = far[i].at[part, :], near[i].at[part, :]
            else:
                part = pl.ds(c * (lanes // cut), lanes // cut)
                a, b = far[i].at[:, part], near[i].at[:, part]
            if i >= len(ins):
                a, b = b, a
            return pltpu.make_async_copy(a, b, sems.at[i, c])

        came = range(first, len(ins))
        sent = range(len(ins), count)
        steps = [PAIRS // cut for cut in pieces]
        for i in came:
            if small[i]:
                copy(i, 0).start()
        for c in range(pieces[0]):
            for i in came:
                if not small[i]:
                    copy(i, c).start()

        def ready(p):
            for i in came:
                if small[i] and names[i] == p:
                    copy(i, 0).wait()
                if not small[i] and p in range(0, PAIRS, steps[0]):
                    copy(i, p // steps[0]).wait()

        def emit(p):
            for i in sent:
                if not small[i] and p % steps[1] == steps[1] - 1:
                    copy(i, p // steps[1]).start()

        kernel(ready, emit, *near, *own)
        for i in sent:
            if small[i]:
                copy(i, 0).start()
        for i in sent:
            for c in range(1 if small[i] else pieces[1]):
                copy(i, c).wait()

    hbm = pl.BlockSpec(memory_space=pltpu.HBM)
    results = [jax.ShapeDtypeStruct(shape, dtype) for shape, dtype in out_shapes]
    size = sum(math.prod(shape) * jnp.dtype(dtype).itemsize for shape, dtype in shapes)
    return pl.pallas_call(
        body,
        out_shape=results,
        in_specs=[pl.BlockSpec(memory_space=pltpu.VMEM) if close else hbm] * len(ins),
        out_specs=[hbm] * len(outs),
        scratch_shapes=[
            *(pltpu.VMEM(shape, dtype) for shape, dtype in shapes[first:]),
            pltpu.SemaphoreType.DMA((count, max(pieces))),
            *(pltpu.VMEM(shape, dtype) for shape, dtype in scratch),
        ],
        cost_estimate=pl.CostEstimate(flops=flops, bytes_accessed=size, transcendentals=0),
        compiler_params=pltpu.CompilerParams(vmem_limit_bytes=limit << 20),
    )(*ins.values())


def exchange(array, axis):
    count = lax.axis_size(axis)
    rows, lanes = array.shape
    pieces = array.reshape(count, 1, rows // count * lanes)
    return lax.all_to_all(pieces, axis, 0, 0, tiled=True).reshape(rows, lanes)


def shards(queries, keys, values, log_decay, gain, d_out):
    length, features = queries.shape[1:]
    heads = log_decay.shape[1]
    pairs = features // LANES
    count = lax.axis_size("seq")
    assert features == 32 * count and features == 64 * heads and length == LANES and pairs == PAIRS
    q, k, v, g, log = queries[0], keys[0], values[0], d_out[0], log_decay[0]
    wide = ((length, features), F32)
    half = ((length, features), BF16)
    small = ((heads, length), F32)
    turned = ((length, heads), F32)
    sent = ((17 * count, LANES), F32)

    (fresh,) = staged(fresh_kernel, 1 << 27, 60, (1, 2), dict(log=log, k=k, v=v), dict(out=sent))
    arrived = exchange(fresh, "seq")
    cum, cum_t, weight, inside = staged(
        inside_kernel, 1 << 30, 60, (2, 1), dict(log=log, q=q, k=k, v=v),
        dict(cum=small, cum_t=turned, weight=turned, inside=((length, features + LANES), F32)),
    )
    arrived, inside = lax.optimization_barrier((arrived, inside))
    begun, decays = call(
        scan_kernel, [((16 * count, LANES), F32), ((count, LANES), F32)], 1 << 20, arrived
    )
    start = exchange(begun, "seq")
    (incoming,) = staged(
        middle_kernel, 1 << 28, 8, (1, 2),
        dict(gain=gain[None], q=q, g=g, state=start, inside=inside),
        dict(out=sent), [wide], close=True,
    )
    returned = exchange(incoming, "seq")
    z, d_queries, dk, dv = staged(
        local_kernel, 1 << 31, 60, (1, 2),
        dict(
            log=log, cum=cum, cum_t=cum_t, gain=gain[None],
            q=q, k=k, v=v, g=g, state=start, inside=inside,
        ),
        dict(z=small, dq=half, dk=wide, dv=wide), [wide, small],
    )
    returned, dk = lax.optimization_barrier((returned, dk))
    (ended,) = call(back_kernel, [sent], 1 << 20, returned, decays)
    ended = exchange(ended, "seq")
    shares = ((lax.axis_size("dp"), pairs, LANES), F32)
    (share,) = call(gain_kernel, [shares], 1 << 10, ended)
    share = lax.all_to_all(share, "dp", 0, 0, tiled=True)
    (d_gain,) = call(gain_sum_kernel, [((pairs, LANES), F32)], 1 << 10, share)
    d_log, d_keys, d_values = staged(
        last_kernel, 1 << 28, 60, (2, 2),
        {"log": log, "z": z, "w": weight, "in": ended, "k": k, "v": v, "s": start, "dk": dk, "dv": dv},
        dict(log=small, dk=half, dv=half), [((heads, LANES), F32)],
    )
    return d_queries[None], d_keys[None], d_values[None], d_log[None], d_gain.reshape(features)


def solution(mesh):
    tokens, decays = P("dp", "seq", None), P("dp", None, "seq")
    return jax.shard_map(
        shards,
        mesh=mesh,
        in_specs=(tokens, tokens, tokens, decays, P(), tokens),
        out_specs=(tokens, tokens, tokens, decays, P()),
        check_vma=False,
    )
```
